128 devices in a mesh: depth: 32 (over x, z, core), stripe: 4 (over y).
Axes of the slice: x: 4, y: 4, z: 4, core: 2. Of those that a mesh axis runs over, the one named last changes fastest.
Arguments:
- object_slices: float32 [32, 2, 1024, 384], P('depth', None, 'stripe'), may hold values from -1 to 1, as said below
- probe_wave: bfloat16 [2, 256, 256], replicated, may hold values from -5 to 5
- amplitudes: bfloat16 [16, 256, 256], P('stripe'), may hold values from 0 to 2
- positions: int32 [16, 2], replicated, may hold values from 0 to 255, as said below
- counts: int32 [4], replicated, may hold values from 1 to 4, as said below
Outputs:
- grad_object: float32 [32, 2, 1024, 384], P('depth', None, 'stripe')
The draws below stay inside these ranges and needn't reach their ends.
Inputs may be any that keep to these rules, and one draw needn't show every extreme that they name: `object_slices`: every cell has magnitude at most 1. `positions`: row offsets lie in 0 to 255 and column offsets in 0 to 128. The counts sum to 8 and the largest equals 4; a stripe's live slots are its first ones.
All inputs are finite; a program needn't handle non-finite values.
Results may differ from the reference program's by a relative error of at most 0.0003.
Values may be sent and summed in bfloat16 or wider, within the bound.
No kernel may reach another device: no remote copies, remote signals or barrier semaphores. Data moves between devices by JAX's collectives and lax.ppermute only.
A program may use at most 64 MiB of HBM per device.

```python
import math
import jax
import jax.numpy as jnp
from jax import lax

WIN = 256
STRIPE_ROWS = 256
W = 384
CAP = 4
SLICES = 32
ROWS_ALL = 1024
SLOTS = 16
TOTAL = 8
N_STRIPE = 4


def draw_object_slices(key, part):
    key_mag, key_phase = jax.random.split(jax.random.fold_in(key, 11))
    shape = (SLICES, ROWS_ALL, W)
    magnitude = jax.random.uniform(key_mag, shape, jnp.float32, 0.97, 1.0)
    phase_angle = jax.random.uniform(key_phase, shape, jnp.float32, -math.pi, math.pi)
    return jnp.stack([magnitude * jnp.cos(phase_angle), magnitude * jnp.sin(phase_angle)], axis=1).astype(jnp.float32)


def draw_positions(key, part):
    key_row, key_col, key_cross = jax.random.split(jax.random.fold_in(key, 23), 3)
    rows_drawn = jax.random.randint(key_row, (SLOTS,), 0, STRIPE_ROWS, jnp.int32)
    cols_drawn = jax.random.randint(key_col, (SLOTS,), 0, W - WIN + 1, jnp.int32)
    crossing = jax.random.randint(key_cross, (N_STRIPE,), STRIPE_ROWS - WIN // 2, STRIPE_ROWS, jnp.int32)
    first_slots = jnp.arange(N_STRIPE, dtype=jnp.int32) * CAP
    rows_drawn = rows_drawn.at[first_slots].set(crossing)
    rows_drawn = rows_drawn.at[0].set(STRIPE_ROWS - 1)
    cols_drawn = cols_drawn.at[0].set(W - WIN).at[1].set(0)
    return jnp.stack([rows_drawn, cols_drawn], axis=1).astype(jnp.int32)


def draw_counts(key, part):
    key_fill, key_turn = jax.random.split(jax.random.fold_in(key, 37))
    spare_units = (N_STRIPE - 1) * (CAP - 1)
    drawn_units = TOTAL - CAP - (N_STRIPE - 1)
    unit_order = jax.random.permutation(key_fill, spare_units)
    chosen = unit_order[:drawn_units] // (CAP - 1)
    added_units = jnp.sum((chosen[:, None] == jnp.arange(N_STRIPE - 1, dtype=jnp.int32)[None, :]).astype(jnp.int32), axis=0)
    rest_counts = (1 + added_units).astype(jnp.int32)
    full_counts = jnp.concatenate([jnp.full((1,), CAP, jnp.int32), rest_counts])
    rotation = jax.random.randint(key_turn, (), 0, N_STRIPE, jnp.int32)
    return jnp.roll(full_counts, rotation).astype(jnp.int32)


def levels(rng, dims, pieces, smallest, largest):
    gain, own = 1.0, jax.random.fold_in(rng, 6)
    for position, blocks in pieces:
        heights = jnp.exp(jax.random.uniform(jax.random.fold_in(own, position), (blocks,), jnp.float32, smallest / len(pieces), largest / len(pieces)))
        gain = gain * jnp.repeat(heights, dims[position] // blocks).reshape([-1 if axis == position else 1 for axis in range(len(dims))])
    return gain


def bell_draw(own_key, extent, scale, most, kind=jnp.bfloat16):
    values = scale * jax.random.normal(own_key, extent, jnp.float32)
    return jnp.clip(values, min=-most, max=most).astype(kind)


def setup_inputs(seed: int = 0) -> dict:
    streams_of = jax.random.split(jax.random.key(seed), 6)
    object_slices = draw_object_slices(jax.random.fold_in(streams_of[5], 71), 0)
    probe_wave = bell_draw(streams_of[1], (2, WIN, WIN), 0.7, 5.0)
    amplitudes = jnp.clip(2.0 * jax.random.uniform(streams_of[2], (SLOTS, WIN, WIN), jnp.float32) ** levels(streams_of[2], (SLOTS, WIN, WIN), ((0, 4),), -0.2, 0.2), 0.0, 2.0).astype(jnp.bfloat16)
    positions = draw_positions(jax.random.fold_in(streams_of[5], 71), 0)
    counts = draw_counts(jax.random.fold_in(streams_of[5], 71), 0)
    return {"object_slices": object_slices, "probe_wave": probe_wave, "amplitudes": amplitudes, "positions": positions, "counts": counts}


smoothing = 0.25
highest = lax.Precision.HIGHEST

def make_tables(length):
    index_row = jnp.arange(length, dtype=jnp.int32)
    product = index_row[:, None] * index_row[None, :] % length
    angle = 2.0 * math.pi * product.astype(jnp.float32) / length
    scale = 1.0 / math.sqrt(length)
    cos_part = (jnp.cos(angle) * scale).astype(jnp.float32)
    sin_part = (-jnp.sin(angle) * scale).astype(jnp.float32)
    neg_part = (jnp.sin(angle) * scale).astype(jnp.float32)
    right_fwd = jnp.concatenate([cos_part, sin_part], axis=1)
    left_fwd = jnp.concatenate([cos_part, sin_part], axis=0)
    right_inv = jnp.concatenate([cos_part, neg_part], axis=1)
    left_inv = jnp.concatenate([cos_part, neg_part], axis=0)
    freq = ((index_row + length // 2) % length - length // 2).astype(jnp.float32)
    phase = -math.pi * (freq[:, None] * freq[:, None] + freq[None, :] * freq[None, :]) / (2.0 * length)
    return (right_fwd, left_fwd, right_inv, left_inv, jnp.cos(phase), jnp.sin(phase))

def transform(real_in, imag_in, right_tab, left_tab):
    length = real_in.shape[0]
    stacked = jnp.concatenate([real_in, imag_in], axis=0)
    first_pass = jnp.dot(stacked, right_tab, precision=highest, preferred_element_type=jnp.float32)
    mid_real = first_pass[:length, :length] - first_pass[length:, length:]
    mid_imag = first_pass[:length, length:] + first_pass[length:, :length]
    second = jnp.dot(left_tab, jnp.concatenate([mid_real, mid_imag], axis=1), precision=highest, preferred_element_type=jnp.float32)
    out_real = second[:length, :length] - second[length:, length:]
    out_imag = second[:length, length:] + second[length:, :length]
    return (out_real, out_imag)

def transmit(wave_in, window):
    real_t = wave_in[0] * window[0] - wave_in[1] * window[1]
    imag_t = wave_in[0] * window[1] + wave_in[1] * window[0]
    return (real_t, imag_t)

def advance(wave_in, window, tables):
    right_fwd, left_fwd, right_inv, left_inv, prop_cos, prop_sin = tables
    real_t, imag_t = transmit(wave_in, window)
    spec_real, spec_imag = transform(real_t, imag_t, right_fwd, left_fwd)
    prop_real = spec_real * prop_cos - spec_imag * prop_sin
    prop_imag = spec_real * prop_sin + spec_imag * prop_cos
    out_real, out_imag = transform(prop_real, prop_imag, right_inv, left_inv)
    return jnp.stack([out_real, out_imag])

def exit_adjoint(wave_in, window, amplitude, tables):
    right_fwd, left_fwd = (tables[0], tables[1])
    real_t, imag_t = transmit(wave_in, window)
    far_real, far_imag = transform(real_t, imag_t, right_fwd, left_fwd)
    smooth = jnp.sqrt(far_real * far_real + far_imag * far_imag + smoothing)
    factor = 1.0 - amplitude.astype(jnp.float32) / smooth
    return jnp.stack([factor * far_real, factor * far_imag])

def unfold(adjoint, tables):
    out_real, out_imag = transform(adjoint[0], adjoint[1], tables[2], tables[3])
    return jnp.stack([out_real, out_imag])

def retreat(adjoint, tables):
    right_fwd, left_fwd, right_inv, left_inv, prop_cos, prop_sin = tables
    spec_real, spec_imag = transform(adjoint[0], adjoint[1], right_fwd, left_fwd)
    back_real = spec_real * prop_cos + spec_imag * prop_sin
    back_imag = spec_imag * prop_cos - spec_real * prop_sin
    out_real, out_imag = transform(back_real, back_imag, right_inv, left_inv)
    return jnp.stack([out_real, out_imag])

def slice_grad(wave_in, middle):
    return jnp.stack([wave_in[0] * middle[0] + wave_in[1] * middle[1], wave_in[0] * middle[1] - wave_in[1] * middle[0]])

def back_wave(window, middle):
    return jnp.stack([window[0] * middle[0] + window[1] * middle[1], window[0] * middle[1] - window[1] * middle[0]])

def reference(object_slices, probe_wave, amplitudes, positions, counts):
    tables = make_tables(WIN)
    total_rows = object_slices.shape[2]
    padded = jnp.concatenate([object_slices, object_slices[:, :, :WIN]], axis=2)
    zero_index = jnp.zeros((), jnp.int32)
    probe_float = probe_wave.astype(jnp.float32)

    def one_slot(gradient, slot_id):
        stripe_id = slot_id // CAP
        is_live = slot_id % CAP < counts[stripe_id]
        row_start = (stripe_id * STRIPE_ROWS + positions[slot_id, 0]).astype(jnp.int32)
        col_start = positions[slot_id, 1].astype(jnp.int32)
        corner = (zero_index, zero_index, row_start, col_start)

        def slot_work(gradient):
            windows = lax.dynamic_slice(padded, corner, (SLICES, 2, WIN, WIN))

            def forward_layer(wave_in, window):
                return (advance(wave_in, window, tables), wave_in)
            last_in, inputs = lax.scan(forward_layer, probe_float, windows[:-1])
            far_adj = exit_adjoint(last_in, windows[-1], amplitudes[slot_id], tables)
            middle = unfold(far_adj, tables)
            grad_last = slice_grad(last_in, middle)
            adjoint = back_wave(windows[-1], middle)

            def backward_layer(adjoint, pair_in):
                window, wave_in = pair_in
                middle = retreat(adjoint, tables)
                return (back_wave(window, middle), slice_grad(wave_in, middle))
            _, slice_grads = lax.scan(backward_layer, adjoint, (windows[:-1], inputs), reverse=True)
            all_grads = jnp.concatenate([slice_grads, grad_last[None]], axis=0)
            region = lax.dynamic_slice(gradient, corner, (SLICES, 2, WIN, WIN))
            return lax.dynamic_update_slice(gradient, region + all_grads, corner)
        return (lax.cond(is_live, slot_work, lambda kept: kept, gradient), None)
    start_grad = jnp.zeros(padded.shape, jnp.float32)
    gradient, _ = lax.scan(one_slot, start_grad, jnp.arange(SLOTS, dtype=jnp.int32))
    head_rows = gradient[:, :, :WIN] + gradient[:, :, total_rows:]
    return jnp.concatenate([head_rows, gradient[:, :, WIN:total_rows]], axis=2)
```

```python
import numpy as np

import jax
import jax.numpy as jnp
from jax import lax
from jax.experimental import pallas as pl
from jax.experimental.pallas import tpu as pltpu
from jax.sharding import PartitionSpec as P

WIN = 256
HALF = 128
ROWS = 256
COLS = 384
CAP = 4
GROUP = 8
STAGES = 4
CHUNK = 64
smoothing = 0.25
f32 = jnp.float32
bf16 = jnp.bfloat16


def split_np(table):
    high = table.astype(bf16)
    low = (table - high.astype(np.float64)).astype(bf16)
    return high, low


def make_tables():
    n = np.arange(HALF)[:, None]
    k = np.arange(HALF)[None, :]
    tables = []
    for parity in (0, 1):
        angle = -2.0 * np.pi * ((n * (2 * k + parity)) % WIN) / WIN
        c, s = np.cos(angle) / 16.0, np.sin(angle) / 16.0
        full = np.block([[c, s], [-s, c]])
        for table in (full, full.T):
            tables.extend(split_np(table))
    dft = np.stack(tables)
    order = np.concatenate([np.arange(0, WIN, 2), np.arange(1, WIN, 2)])
    freq = (((order + HALF) % WIN) - HALF).astype(np.float64)
    phase = -np.pi * (freq[:, None] ** 2 + freq[None, :] ** 2) / (2.0 * WIN)
    fresnel = np.stack([np.cos(phase), np.sin(phase)]).astype(np.float32)
    pick = np.zeros((WIN, WIN))
    pick[np.arange(WIN), order] = 1.0
    return dft, fresnel, np.stack([pick, pick.T]).astype(bf16)


EVEN, EVEN_T, ODD, ODD_T = 0, 2, 4, 6


def halves(value):
    high = value.astype(bf16)
    low = (value - high.astype(f32)).astype(bf16)
    return high, low


def mm(a, b):
    return jnp.dot(a, b, preferred_element_type=f32)


def right_mul(data, dft, which):
    high, low = halves(data)
    return mm(high, dft[which]) + mm(low, dft[which]) + mm(high, dft[which + 1])


def left_mul(dft, which, data):
    high, low = halves(data)
    return mm(dft[which], high) + mm(dft[which], low) + mm(dft[which + 1], high)


def lanes(a, b):
    return jnp.concatenate([a, b], axis=1)


def rows(a, b):
    return jnp.concatenate([a, b], axis=0)


def propagate(source, sink, dft, mid, pointwise):
    for start in range(0, WIN, CHUNK):
        part = slice(start, start + CHUNK)
        re, im = source(part)
        even = lanes(re[:, :HALF] + re[:, HALF:], im[:, :HALF] + im[:, HALF:])
        odd = lanes(re[:, :HALF] - re[:, HALF:], im[:, :HALF] - im[:, HALF:])
        even = right_mul(even, dft, EVEN)
        odd = right_mul(odd, dft, ODD)
        mid[0, part, :] = lanes(even[:, :HALF], odd[:, :HALF])
        mid[1, part, :] = lanes(even[:, HALF:], odd[:, HALF:])
    re_top, re_low = mid[0, :HALF, :], mid[0, HALF:, :]
    im_top, im_low = mid[1, :HALF, :], mid[1, HALF:, :]
    even = left_mul(dft, EVEN_T, rows(re_top + re_low, im_top + im_low))
    odd = left_mul(dft, ODD_T, rows(re_top - re_low, im_top - im_low))
    even = pointwise(slice(0, HALF), even[:HALF], even[HALF:])
    odd = pointwise(slice(HALF, WIN), odd[:HALF], odd[HALF:])
    even = left_mul(dft, EVEN, rows(*even))
    odd = left_mul(dft, ODD, rows(*odd))
    mid[0, :HALF, :] = even[:HALF] + odd[:HALF]
    mid[0, HALF:, :] = even[:HALF] - odd[:HALF]
    mid[1, :HALF, :] = even[HALF:] + odd[HALF:]
    mid[1, HALF:, :] = even[HALF:] - odd[HALF:]
    for start in range(0, WIN, CHUNK):
        part = slice(start, start + CHUNK)
        re, im = mid[0, part, :], mid[1, part, :]
        even = right_mul(lanes(re[:, :HALF], im[:, :HALF]), dft, EVEN_T)
        odd = right_mul(lanes(re[:, HALF:], im[:, HALF:]), dft, ODD_T)
        total, diff = even + odd, even - odd
        sink(part, lanes(total[:, :HALF], diff[:, :HALF]), lanes(total[:, HALF:], diff[:, HALF:]))


def fresnel_times(fresnel, sign):
    def pointwise(part, re, im):
        c, s = fresnel[0, part, :], fresnel[1, part, :]
        if sign > 0:
            return re * c - im * s, re * s + im * c
        return re * c + im * s, im * c - re * s

    return pointwise


def forward_kernel(last, flag, wave_in, win_re, win_im, dft, fresnel, *rest):
    if last:
        pattern, pick, wave_out, stored, wave, mid, far_amp = rest
    else:
        wave_out, stored, wave, mid = rest
    step = pl.program_id(0)

    @pl.when(flag[0] == 1)
    def _():
        @pl.when(step == 0)
        def _():
            wave[...] = wave_in[...].astype(f32)
            if last:
                picked = mm(pick[0], pattern[...]).astype(bf16)
                far_amp[...] = mm(picked, pick[1])

        stored[0] = wave[...]

        def source(part):
            wr, wi = wave[0, part, :], wave[1, part, :]
            tr, ti = win_re[0, part, :], win_im[0, part, :]
            return wr * tr - wi * ti, wr * ti + wi * tr

        def sink(part, re, im):
            wave[0, part, :] = re
            wave[1, part, :] = im

        def sink_out(part, re, im):
            wave_out[0, part, :] = re
            wave_out[1, part, :] = im

        def exit_point(part, re, im):
            smooth = jnp.sqrt(re * re + im * im + smoothing)
            factor = 1.0 - far_amp[part, :] / smooth
            return factor * re, factor * im

        if last:
            @pl.when(step < GROUP - 1)
            def _():
                propagate(source, sink, dft, mid, fresnel_times(fresnel, 1))

            @pl.when(step == GROUP - 1)
            def _():
                propagate(source, sink_out, dft, mid, exit_point)
        else:
            propagate(source, sink, dft, mid, fresnel_times(fresnel, 1))

            @pl.when(step == GROUP - 1)
            def _():
                wave_out[...] = wave[...]


def forward_stage(last, flag, wave, win_re, win_im, dft, fresnel, pattern=None, pick=None):
    whole = lambda *shape: pl.BlockSpec(shape, lambda i, flag: (0,) * len(shape))
    one = pl.BlockSpec((1, WIN, WIN), lambda i, flag: (i * flag[0], 0, 0))
    args = [wave, win_re, win_im, dft, fresnel]
    specs = [whole(2, WIN, WIN), one, one, whole(8, WIN, WIN), whole(2, WIN, WIN)]
    scratch = [pltpu.VMEM((2, WIN, WIN), f32), pltpu.VMEM((2, WIN, WIN), f32)]
    if last:
        args += [pattern, pick]
        specs += [whole(WIN, WIN), whole(2, WIN, WIN)]
        scratch += [pltpu.VMEM((WIN, WIN), f32)]
    return pl.pallas_call(
        lambda *refs: forward_kernel(last, *refs),
        grid_spec=pltpu.PrefetchScalarGridSpec(
            num_scalar_prefetch=1,
            grid=(GROUP,),
            in_specs=specs,
            out_specs=[
                whole(2, WIN, WIN),
                pl.BlockSpec((1, 2, WIN, WIN), lambda i, flag: (i * flag[0], 0, 0, 0)),
            ],
            scratch_shapes=scratch,
        ),
        out_shape=[
            jax.ShapeDtypeStruct((2, WIN, WIN), f32),
            jax.ShapeDtypeStruct((GROUP, 2, WIN, WIN), f32),
        ],
        compiler_params=pltpu.CompilerParams(vmem_limit_bytes=40 * 2**20),
        name="forward_last" if last else "forward_stage",
    )(flag, *args)


def backward_kernel(last, flag, adj_in, win_re, win_im, stored, dft, fresnel, grad_in,
                    adj_out, grad, adj, mid, grad_buf, sem):
    del grad_in
    step = pl.program_id(0)
    slot = lax.rem(step, 2)

    def grad_copy(slot_id, slice_id):
        return pltpu.make_async_copy(grad_buf.at[slot_id], grad.at[:, slice_id], sem.at[slot_id])

    @pl.when(flag[0] == 1)
    def _():
        @pl.when(step >= 2)
        def _():
            grad_copy(slot, GROUP - 1 - (step - 2)).wait()

        def finish(part, mr, mi):
            wr, wi = stored[0, 0, part, :], stored[0, 1, part, :]
            grad_buf[slot, 0, part, :] = wr * mr + wi * mi
            grad_buf[slot, 1, part, :] = wr * mi - wi * mr
            tr, ti = win_re[0, part, :], win_im[0, part, :]
            adj[0, part, :] = tr * mr + ti * mi
            adj[1, part, :] = tr * mi - ti * mr

        def source(part):
            return adj[0, part, :], adj[1, part, :]

        if last:
            @pl.when(step == 0)
            def _():
                for start in range(0, WIN, CHUNK):
                    part = slice(start, start + CHUNK)
                    finish(part, adj_in[0, part, :], adj_in[1, part, :])

            @pl.when(step > 0)
            def _():
                propagate(source, finish, dft, mid, fresnel_times(fresnel, -1))
        else:
            @pl.when(step == 0)
            def _():
                adj[...] = adj_in[...]

            propagate(source, finish, dft, mid, fresnel_times(fresnel, -1))

        grad_copy(slot, GROUP - 1 - step).start()

        @pl.when(step == GROUP - 1)
        def _():
            adj_out[...] = adj[...]
            grad_copy(1 - slot, 1).wait()
            grad_copy(slot, 0).wait()


def backward_stage(last, flag, adj, win_re, win_im, stored, dft, fresnel, grad):
    whole = lambda *shape: pl.BlockSpec(shape, lambda i, flag: (0,) * len(shape))
    one = pl.BlockSpec((1, WIN, WIN), lambda i, flag: ((GROUP - 1 - i) * flag[0], 0, 0))
    return pl.pallas_call(
        lambda *refs: backward_kernel(last, *refs),
        grid_spec=pltpu.PrefetchScalarGridSpec(
            num_scalar_prefetch=1,
            grid=(GROUP,),
            in_specs=[
                whole(2, WIN, WIN),
                one,
                one,
                pl.BlockSpec((1, 2, WIN, WIN), lambda i, flag: ((GROUP - 1 - i) * flag[0], 0, 0, 0)),
                whole(8, WIN, WIN),
                whole(2, WIN, WIN),
                pl.BlockSpec(memory_space=pl.ANY),
            ],
            out_specs=[whole(2, WIN, WIN), pl.BlockSpec(memory_space=pl.ANY)],
            scratch_shapes=[
                pltpu.VMEM((2, WIN, WIN), f32),
                pltpu.VMEM((2, WIN, WIN), f32),
                pltpu.VMEM((2, 2, WIN, WIN), f32),
                pltpu.SemaphoreType.DMA((2,)),
            ],
        ),
        out_shape=[
            jax.ShapeDtypeStruct((2, WIN, WIN), f32),
            jax.ShapeDtypeStruct((2, GROUP, WIN, WIN), f32),
        ],
        input_output_aliases={7: 1},
        compiler_params=pltpu.CompilerParams(vmem_limit_bytes=40 * 2**20),
        name="backward_last" if last else "backward_stage",
    )(flag, adj, win_re, win_im, stored, dft, fresnel, grad)


def corner(place, slot):
    row, col = place[slot, 0], place[slot, 1]
    base = pl.multiple_of((row >> 3) << 3, 8)
    return base, row - base, col


def cut_kernel(place, own, after, out, slab):
    slab[:, :ROWS, :] = own[0]
    slab[:, ROWS:, :] = after[0]
    for slot in range(CAP):
        base, shift, col = corner(place, slot)
        for comp in range(2):
            picked = slab[comp, pl.ds(base, WIN + 8), :]
            picked = pltpu.roll(picked, lax.rem(COLS - col, COLS), 1)[:, :WIN]
            out[2 * slot + comp] = pltpu.roll(picked, lax.rem(WIN + 8 - shift, WIN + 8), 0)[:WIN]


def cut_windows(place, own, after):
    vmem = pl.BlockSpec(memory_space=pltpu.VMEM)
    return pl.pallas_call(
        cut_kernel,
        in_specs=[pl.BlockSpec(memory_space=pltpu.SMEM), vmem, vmem],
        out_specs=vmem,
        out_shape=jax.ShapeDtypeStruct((2 * CAP, WIN, WIN), f32),
        scratch_shapes=[pltpu.VMEM((2, 2 * ROWS, COLS), f32)],
        compiler_params=pltpu.CompilerParams(vmem_limit_bytes=40 * 2**20),
        name="cut_windows",
    )(place, own, after)


def add_kernel(place, live, grads, top, low, slab):
    slab[...] = jnp.zeros_like(slab)
    for slot in range(CAP):
        base, shift, col = corner(place, slot)

        @pl.when(slot < live[0])
        def _():
            for comp in range(2):
                tall = rows(grads[2 * slot + comp], jnp.zeros((8, WIN), f32))
                tall = pltpu.roll(tall, shift, 0)
                wide = lanes(tall, jnp.zeros((WIN + 8, COLS - WIN), f32))
                slab[comp, pl.ds(base, WIN + 8), :] += pltpu.roll(wide, col, 1)
    top[0] = slab[:, :ROWS, :]
    low[0] = slab[:, ROWS:, :]


def add_windows(place, live, grads):
    vmem = pl.BlockSpec(memory_space=pltpu.VMEM)
    smem = pl.BlockSpec(memory_space=pltpu.SMEM)
    shape = jax.ShapeDtypeStruct((1, 2, ROWS, COLS), f32)
    return pl.pallas_call(
        add_kernel,
        in_specs=[smem, smem, vmem],
        out_specs=[vmem, vmem],
        out_shape=[shape, shape],
        scratch_shapes=[pltpu.VMEM((2, 2 * ROWS, COLS), f32)],
        compiler_params=pltpu.CompilerParams(vmem_limit_bytes=40 * 2**20),
        name="add_windows",
    )(place, live, grads)


def device(x, z, core):
    return x * GROUP + z * 2 + core


ring = range(4)
rings = [[x * GROUP + i for i in range(GROUP)] for x in ring]


def body(object_slices, probe_wave, amplitudes, positions, counts):
    depth = lax.axis_index("depth")
    stripe = lax.axis_index("stripe")
    stage = depth // GROUP
    slot = (depth % GROUP) // 2
    core = depth % 2
    dft, fresnel, pick = (jnp.asarray(t) for t in make_tables())
    place = lax.dynamic_slice_in_dim(positions, stripe * CAP, CAP, 0)
    live = lax.dynamic_slice_in_dim(counts, stripe, 1, 0)
    works = (core == 0) & (slot < live[0])

    def flag_of(t):
        return (works & (stage == t)).astype(jnp.int32)[None]

    after = lax.ppermute(object_slices, "stripe", [(i, (i - 1) % 4) for i in ring])
    windows = cut_windows(place, object_slices, after)
    mine = lax.all_to_all(windows, "depth", 0, 0, axis_index_groups=rings, tiled=True)
    win_im = lax.ppermute(mine, "depth", [(device(x, z, 1), device(x, z, 0)) for x in ring for z in ring])
    win_re = mine

    pattern = lax.dynamic_index_in_dim(amplitudes, slot, 0, keepdims=False)
    wave = probe_wave
    stored = []
    for t in range(STAGES):
        last = t == STAGES - 1
        extra = (pattern, pick) if last else ()
        wave, kept = forward_stage(last, flag_of(t), wave, win_re, win_im, dft, fresnel, *extra)
        stored.append(kept)
        if not last:
            wave = lax.ppermute(wave, "depth", [(device(t, z, 0), device(t + 1, z, 0)) for z in ring])
    grad = jnp.zeros((2, GROUP, WIN, WIN), f32)
    for t in reversed(range(STAGES)):
        last = t == STAGES - 1
        wave, grad = backward_stage(
            last, flag_of(t), wave, win_re, win_im, stored[t], dft, fresnel, grad
        )
        if t > 0:
            wave = lax.ppermute(wave, "depth", [(device(t, z, 0), device(t - 1, z, 0)) for z in ring])
    grad_im = lax.ppermute(
        grad[1], "depth", [(device(x, z, 0), device(x, z, 1)) for x in ring for z in ring]
    )
    outgoing = jnp.where(core == 0, grad[0], grad_im)
    back = lax.all_to_all(outgoing, "depth", 0, 0, axis_index_groups=rings, tiled=True)
    top, low = add_windows(place, live, back)
    return top + lax.ppermute(low, "stripe", [(i, (i + 1) % 4) for i in ring])


def solution(mesh):
    return jax.shard_map(
        body,
        mesh=mesh,
        in_specs=(P("depth", None, "stripe", None), P(), P("stripe", None, None), P(), P()),
        out_specs=P("depth", None, "stripe", None),
        check_vma=False,
    )
```

```python
import numpy as np

import jax
import jax.numpy as jnp
from jax import lax
from jax.experimental import pallas as pl
from jax.experimental.pallas import tpu as pltpu
from jax.sharding import PartitionSpec as P

WIN = 256
HALF = 128
ROWS = 256
COLS = 384
CAP = 4
GROUP = 8
STAGES = 4
CHUNK = 128
smoothing = 0.25
f32 = jnp.float32
bf16 = jnp.bfloat16


def split_np(table):
    high = table.astype(bf16)
    low = (table - high.astype(np.float64)).astype(bf16)
    return high, low


def make_tables():
    n = np.arange(HALF)[:, None]
    k = np.arange(HALF)[None, :]
    tables = []
    for parity in (0, 1):
        angle = -2.0 * np.pi * ((n * (2 * k + parity)) % WIN) / WIN
        c, s = np.cos(angle) / 16.0, np.sin(angle) / 16.0
        full = np.block([[c, s], [-s, c]])
        for table in (full, full.T):
            tables.extend(split_np(table))
    dft = np.stack(tables)
    freq = (((np.arange(WIN) + HALF) % WIN) - HALF).astype(np.float64)
    response = np.fft.ifft(np.exp(-1j * np.pi * freq**2 / (2.0 * WIN)))
    near = response[(n - k) % WIN]
    far = response[(n - k - HALF) % WIN]
    tables = []
    for block in ((near + far) / 2.0, (near - far) / 2.0):
        tables.extend(split_np(np.block([[block.real, block.imag], [-block.imag, block.real]])))
    chirp = np.stack(tables)
    order = np.concatenate([np.arange(0, WIN, 2), np.arange(1, WIN, 2)])
    pick = np.zeros((WIN, WIN))
    pick[np.arange(WIN), order] = 1.0
    return dft, chirp, np.stack([pick, pick.T]).astype(bf16)


SUM, DIFF = 0, 2
EVEN, EVEN_T, ODD, ODD_T = 0, 2, 4, 6


def halves(value):
    high = value.astype(bf16)
    low = (value - high.astype(f32)).astype(bf16)
    return high, low


def mm(a, b):
    return jnp.dot(a, b, preferred_element_type=f32)


def right_mul(data, dft, which):
    high, low = halves(data)
    return mm(high, dft[which]) + mm(low, dft[which]) + mm(high, dft[which + 1])


def left_mul(dft, which, data):
    high, low = halves(data)
    return mm(dft[which], high) + mm(dft[which], low) + mm(dft[which + 1], high)


def lanes(a, b):
    return jnp.concatenate([a, b], axis=1)


def rows(a, b):
    return jnp.concatenate([a, b], axis=0)


def propagate(source, sink, chirp):
    top, low = slice(0, HALF), slice(HALF, WIN)
    re_top, im_top = source(top)
    re_low, im_low = source(low)

    sr, si, dr, di = re_top + re_low, im_top + im_low, re_top - re_low, im_top - im_low
    re, im = rows(sr, dr), rows(si, di)
    scol = right_mul(lanes(re[:, :HALF] + re[:, HALF:], im[:, :HALF] + im[:, HALF:]), chirp, SUM)
    dcol = right_mul(lanes(re[:, :HALF] - re[:, HALF:], im[:, :HALF] - im[:, HALF:]), chirp, DIFF)
    im, re = lanes(scol[:, HALF:], dcol[:, HALF:]), lanes(scol[:, :HALF], dcol[:, :HALF])
    total = left_mul(chirp, SUM, rows(im[:HALF], re[:HALF]))
    diff = left_mul(chirp, DIFF, rows(im[HALF:], re[HALF:]))
    for part, both in ((top, total + diff), (low, total - diff)):
        im, re = both[:HALF], both[HALF:]
        sink(
            part,
            lanes(re[:, :HALF] + re[:, HALF:], re[:, :HALF] - re[:, HALF:]),
            lanes(im[:, :HALF] + im[:, HALF:], im[:, :HALF] - im[:, HALF:]),
        )


def exit_wave(source, sink, dft, mid, pointwise):
    for start in range(0, WIN, CHUNK):
        part = slice(start, start + CHUNK)
        re, im = source(part)
        even = lanes(re[:, :HALF] + re[:, HALF:], im[:, :HALF] + im[:, HALF:])
        odd = lanes(re[:, :HALF] - re[:, HALF:], im[:, :HALF] - im[:, HALF:])
        even = right_mul(even, dft, EVEN)
        odd = right_mul(odd, dft, ODD)
        mid[0, part, :] = lanes(even[:, :HALF], odd[:, :HALF])
        mid[1, part, :] = lanes(even[:, HALF:], odd[:, HALF:])
    re_top, re_low = mid[0, :HALF, :], mid[0, HALF:, :]
    im_top, im_low = mid[1, :HALF, :], mid[1, HALF:, :]
    even = left_mul(dft, EVEN_T, rows(re_top + re_low, im_top + im_low))
    odd = left_mul(dft, ODD_T, rows(re_top - re_low, im_top - im_low))
    even = pointwise(slice(0, HALF), even[:HALF], even[HALF:])
    odd = pointwise(slice(HALF, WIN), odd[:HALF], odd[HALF:])
    even = left_mul(dft, EVEN, rows(*even))
    odd = left_mul(dft, ODD, rows(*odd))
    mid[0, :HALF, :] = even[:HALF] + odd[:HALF]
    mid[0, HALF:, :] = even[:HALF] - odd[:HALF]
    mid[1, :HALF, :] = even[HALF:] + odd[HALF:]
    mid[1, HALF:, :] = even[HALF:] - odd[HALF:]
    for start in range(0, WIN, CHUNK):
        part = slice(start, start + CHUNK)
        re, im = mid[0, part, :], mid[1, part, :]
        even = right_mul(lanes(re[:, :HALF], im[:, :HALF]), dft, EVEN_T)
        odd = right_mul(lanes(re[:, HALF:], im[:, HALF:]), dft, ODD_T)
        total, diff = even + odd, even - odd
        sink(part, lanes(total[:, :HALF], diff[:, :HALF]), lanes(total[:, HALF:], diff[:, HALF:]))


CODED = WIN + 16
i16 = jnp.int16


def exponent(most):
    return jnp.ceil(jnp.log2(jnp.maximum(most, 1e-30)))


def encode(dst, part, value):
    exp = exponent(jnp.max(jnp.abs(value), axis=0, keepdims=True))
    scaled = jnp.clip(jnp.round(value * jnp.exp2(15.0 - exp)), -32767.0, 32767.0)
    dst[part, :] = scaled.astype(jnp.int32).astype(i16)
    return jnp.broadcast_to(exp, (8, value.shape[1])).astype(jnp.int32)


def encode_tail(dst, top, low):
    dst[WIN:, :] = jnp.concatenate([top, low], axis=0).astype(i16)


def decode(src, part):
    tail = src[WIN:, :].astype(jnp.int32)[8 * (part.start // HALF):][:1].astype(f32)
    return src[part, :].astype(jnp.int32).astype(f32) * jnp.exp2(tail - 15.0)


TOP, LOW = slice(0, HALF), slice(HALF, WIN)


def encode_plane(dst, top, low):
    encode_tail(dst, encode(dst, TOP, top), encode(dst, LOW, low))


def decode_wave(dst, src):
    for comp in range(2):
        for part in (TOP, LOW):
            dst[comp, part, :] = decode(src.at[comp], part)


def encode_wave(dst, src):
    for comp in range(2):
        encode_plane(dst.at[comp], src[comp, TOP, :], src[comp, LOW, :])


def times(re, im, win, slot, part):
    tr, ti = win[slot, 0, part, :], win[slot, 1, part, :]
    return re * tr - im * ti, re * ti + im * tr


class Windows:
    def __init__(self, piles, buf, sem):
        self.piles, self.buf, self.sem = piles, buf, sem

    def copies(self, i, odd):
        return [
            pltpu.make_async_copy(self.piles[2 * odd + comp].at[i >> 1], self.buf.at[odd, comp], self.sem.at[odd, comp])
            for comp in range(2)
        ]

    def start(self, i):
        for odd in range(2):
            @pl.when((i & 1) == odd)
            def _():
                for copy in self.copies(i, odd):
                    copy.start()

    def wait(self, i):
        for comp in range(2):
            pltpu.make_async_copy(
                self.piles[comp].at[i >> 1], self.buf.at[i & 1, comp], self.sem.at[i & 1, comp]
            ).wait()


def forward_slice(src, dst, windows, i, chirp):
    def source(part):
        return times(src[0, part, :], src[1, part, :], windows.buf, i & 1, part)

    def sink(part, re, im):
        dst[0, part, :] = re
        dst[1, part, :] = im

    propagate(source, sink, chirp)


def retreat(i, part, re, im, adj, wave, windows, grad, tails):
    wr, wi = wave[0, part, :], wave[1, part, :]
    half = part.start // HALF
    for comp, value in enumerate((wr * re - wi * im, -(wr * im + wi * re))):
        tails[comp, 8 * half:8 * half + 8, :] = encode(grad.at[comp], part, value)
    adj[0, part, :], adj[1, part, :] = times(re, im, windows.buf, i & 1, part)


def finish_grad(grad, tails):
    for comp in range(2):
        grad[comp, WIN:, :] = tails[comp].astype(i16)


def backward_slice(i, adj, wave, windows, chirp, grad, tails):
    def source(part):
        return adj[0, part, :], adj[1, part, :]

    def sink(part, re, im):
        retreat(i, part, re, im, adj, wave, windows, grad, tails)

    propagate(source, sink, chirp)
    finish_grad(grad, tails)


def copy_wave(dst, src):
    for comp in range(2):
        dst[comp] = src[comp].astype(f32)


def forward_kernel(first, flag, wave_in, er, ei, orr, oi, chirp, *rest):
    wave_out, waves, win_buf, win_sem, buf, sem = rest[-6:]
    windows = Windows((er, ei, orr, oi), win_buf, win_sem)

    def store(i):
        slot = lax.rem(i, 3)
        return pltpu.make_async_copy(buf.at[slot], waves.at[i], sem.at[slot])

    @pl.when(flag[0] == 1)
    def _():
        windows.start(jnp.int32(0))
        if first:
            copy_wave(buf.at[0], wave_in)
        else:
            decode_wave(buf.at[0], wave_in)

        @pl.loop(0, GROUP)
        def _(i):
            @pl.when(i + 1 < GROUP)
            def _():
                windows.start(i + 1)

            store(i).start()

            @pl.when(i >= 2)
            def _():
                store(i - 2).wait()

            windows.wait(i)
            forward_slice(buf.at[lax.rem(i, 3)], buf.at[lax.rem(i + 1, 3)], windows, i, chirp)

        encode_wave(wave_out, buf.at[GROUP % 3])
        store(jnp.int32(GROUP - 2)).wait()
        store(jnp.int32(GROUP - 1)).wait()


class Gradients:
    def __init__(self, grads, buf, sem):
        self.grads, self.buf, self.sem = grads, buf, sem

    def copies(self, i):
        slot = i & 1
        return [
            pltpu.make_async_copy(self.buf.at[slot, comp], self.grads.at[comp, slot, i >> 1], self.sem.at[slot, comp])
            for comp in range(2)
        ]

    def start(self, i):
        for copy in self.copies(i):
            copy.start()

    def wait(self, i):
        for copy in self.copies(i):
            copy.wait()


def turn_kernel(flag, wave_in, er, ei, orr, oi, chirp, dft, pattern, pick, adj_out, grads,
                win_buf, win_sem, grad_buf, grad_sem, adj, tails, waves, mid, far_amp):
    windows = Windows((er, ei, orr, oi), win_buf, win_sem)
    out = Gradients(grads, grad_buf, grad_sem)
    end = GROUP - 1

    @pl.when(flag[0] == 1)
    def _():
        windows.start(jnp.int32(0))
        picked = mm(pick[0], pattern[...]).astype(bf16)
        far_amp[...] = mm(picked, pick[1])
        decode_wave(waves.at[0], wave_in)

        @pl.loop(0, end)
        def _(i):
            windows.start(i + 1)
            windows.wait(i)
            forward_slice(waves.at[i], waves.at[i + 1], windows, i, chirp)

        windows.wait(jnp.int32(end))
        windows.start(jnp.int32(end - 1))

        def source(part):
            return times(waves[end, 0, part, :], waves[end, 1, part, :], win_buf, end & 1, part)

        def exit_point(part, re, im):
            smooth = jnp.sqrt(re * re + im * im + smoothing)
            factor = 1.0 - far_amp[part, :] / smooth
            return factor * re, factor * im

        def sink(part, re, im):
            retreat(end, part, re, -im, adj, waves.at[end], windows, grad_buf.at[end & 1], tails)

        exit_wave(source, sink, dft, mid, exit_point)
        finish_grad(grad_buf.at[end & 1], tails)
        out.start(jnp.int32(end))

        @pl.loop(0, end)
        def _(step):
            i = end - 1 - step
            windows.wait(i)

            @pl.when(i > 0)
            def _():
                windows.start(i - 1)

            @pl.when(step > 0)
            def _():
                out.wait(i + 2)

            backward_slice(i, adj, waves.at[i], windows, chirp, grad_buf.at[i & 1], tails)
            out.start(i)

        encode_wave(adj_out, adj)
        out.wait(jnp.int32(1))
        out.wait(jnp.int32(0))


def backward_kernel(flag, adj_in, er, ei, orr, oi, chirp, waves, grads_in, adj_out, grads,
                    win_buf, win_sem, grad_buf, grad_sem, adj, tails, wave_buf, wave_sem):
    del grads_in
    windows = Windows((er, ei, orr, oi), win_buf, win_sem)
    out = Gradients(grads, grad_buf, grad_sem)

    def load(i):
        return pltpu.make_async_copy(waves.at[i], wave_buf.at[i & 1], wave_sem.at[i & 1])

    @pl.when(flag[0] == 1)
    def _():
        windows.start(jnp.int32(GROUP - 1))
        load(jnp.int32(GROUP - 1)).start()
        decode_wave(adj, adj_in)

        @pl.loop(0, GROUP)
        def _(step):
            i = GROUP - 1 - step
            windows.wait(i)
            load(i).wait()

            @pl.when(i > 0)
            def _():
                windows.start(i - 1)
                load(i - 1).start()

            @pl.when(step >= 2)
            def _():
                out.wait(i + 2)

            backward_slice(i, adj, wave_buf.at[i & 1], windows, chirp, grad_buf.at[i & 1], tails)
            out.start(i)

        encode_wave(adj_out, adj)
        out.wait(jnp.int32(1))
        out.wait(jnp.int32(0))


vmem = pl.BlockSpec(memory_space=pltpu.VMEM)
smem = pl.BlockSpec(memory_space=pltpu.SMEM)
hbm = pl.BlockSpec(memory_space=pltpu.HBM)
params = pltpu.CompilerParams(vmem_limit_bytes=20 * 2**20)
wave_shape = jax.ShapeDtypeStruct((2, CODED, WIN), i16)
waves_shape = pltpu.HBM((GROUP, 2, WIN, WIN), f32)
grads_shape = pltpu.HBM((2, 2, GROUP // 2, CODED, WIN), i16)
pair = lambda: [pltpu.VMEM((2, 2, WIN, WIN), f32), pltpu.SemaphoreType.DMA((2, 2))]
grad_scratch = lambda: [
    pltpu.VMEM((2, 2, CODED, WIN), i16),
    pltpu.SemaphoreType.DMA((2, 2)),
    pltpu.VMEM((2, WIN, WIN), f32),
    pltpu.VMEM((2, 16, WIN), jnp.int32),
]


def forward_stage(flag, wave, wins, chirp, waves):
    first = waves is None
    args = [flag, wave, *wins, chirp] + ([] if first else [waves])
    return pl.pallas_call(
        lambda *refs: forward_kernel(first, *refs),
        in_specs=[smem, vmem] + [hbm] * 4 + [vmem] + ([] if first else [hbm]),
        out_specs=[vmem, hbm],
        out_shape=[wave_shape, waves_shape],
        input_output_aliases={} if first else {7: 1},
        scratch_shapes=pair() + [pltpu.VMEM((3, 2, WIN, WIN), f32), pltpu.SemaphoreType.DMA((3,))],
        compiler_params=params,
        name="forward_stage",
    )(*args)


def turn_stage(flag, wave, wins, chirp, dft, pattern, pick):
    return pl.pallas_call(
        turn_kernel,
        in_specs=[smem, vmem] + [hbm] * 4 + [vmem] * 4,
        out_specs=[vmem, hbm],
        out_shape=[wave_shape, grads_shape],
        scratch_shapes=pair() + grad_scratch() + [
            pltpu.VMEM((GROUP, 2, WIN, WIN), f32),
            pltpu.VMEM((2, WIN, WIN), f32),
            pltpu.VMEM((WIN, WIN), f32),
        ],
        compiler_params=params,
        name="turn_stage",
    )(flag, wave, *wins, chirp, dft, pattern, pick)


def backward_stage(flag, adj, wins, chirp, waves, grads):
    return pl.pallas_call(
        backward_kernel,
        in_specs=[smem, vmem] + [hbm] * 4 + [vmem, hbm, hbm],
        out_specs=[vmem, hbm],
        out_shape=[wave_shape, grads_shape],
        input_output_aliases={8: 1},
        scratch_shapes=pair() + grad_scratch() + [pltpu.VMEM((2, 2, WIN, WIN), f32), pltpu.SemaphoreType.DMA((2,))],
        compiler_params=params,
        name="backward_stage",
    )(flag, adj, *wins, chirp, waves, grads)


def corner(place, slot):
    row, col = place[slot, 0], place[slot, 1]
    base = pl.multiple_of((row >> 3) << 3, 8)
    return base, row - base, col


def cut_kernel(place, own, after, out, slab):
    slab[:ROWS, :] = own[...]
    slab[ROWS:, :] = after[...]
    for slot in range(CAP):
        base, shift, col = corner(place, slot)
        picked = slab[pl.ds(base, WIN + 8), :]
        picked = pltpu.roll(picked, lax.rem(COLS - col, COLS), 1)[:, :WIN]
        out[slot] = pltpu.roll(picked, lax.rem(WIN + 8 - shift, WIN + 8), 0)[:WIN]


def cut_windows(place, own, after):
    return pl.pallas_call(
        cut_kernel,
        in_specs=[smem, vmem, vmem],
        out_specs=vmem,
        out_shape=jax.ShapeDtypeStruct((CAP, WIN, WIN), f32),
        scratch_shapes=[pltpu.VMEM((2 * ROWS, COLS), f32)],
        compiler_params=params,
        name="cut_windows",
    )(place, own, after)


def add_kernel(place, live, grads, top, low, slab):
    slab[...] = jnp.zeros_like(slab)
    for slot in range(CAP):
        base, shift, col = corner(place, slot)

        @pl.when(slot < live[0])
        def _():
            own = grads.at[slot]
            tall = jnp.concatenate([decode(own, TOP), decode(own, LOW), jnp.zeros((8, WIN), f32)], axis=0)
            tall = pltpu.roll(tall, shift, 0)
            wide = lanes(tall, jnp.zeros((WIN + 8, COLS - WIN), f32))
            slab[pl.ds(base, WIN + 8), :] += pltpu.roll(wide, col, 1)
    top[...] = slab[:ROWS, :]
    encode_plane(low, slab[ROWS:ROWS + HALF, :], slab[ROWS + HALF:, :])


def add_windows(place, live, grads):
    return pl.pallas_call(
        add_kernel,
        in_specs=[smem, smem, vmem],
        out_specs=[vmem, vmem],
        out_shape=[jax.ShapeDtypeStruct((ROWS, COLS), f32), jax.ShapeDtypeStruct((CODED, COLS), i16)],
        scratch_shapes=[pltpu.VMEM((2 * ROWS, COLS), f32)],
        compiler_params=params,
        name="add_windows",
    )(place, live, grads)


def join_kernel(top_re, low_re, top_im, low_im, out):
    for comp, (top, low) in enumerate(((top_re, low_re), (top_im, low_im))):
        for part in (TOP, LOW):
            out[0, comp, part, :] = top[part, :] + decode(low, part)


def join(parts):
    return pl.pallas_call(
        join_kernel,
        in_specs=[vmem] * 4,
        out_specs=vmem,
        out_shape=jax.ShapeDtypeStruct((1, 2, ROWS, COLS), f32),
        compiler_params=params,
        name="join",
    )(*parts)


def device(x, z, core):
    return x * GROUP + z * 2 + core


ring = range(4)
rings = [[device(x, z, core) for z in ring] for x in ring for core in range(2)]


def after_that(value, *earlier):
    return lax.optimization_barrier((value, *earlier))[0]


def exchange(value):
    return lax.all_to_all(value, "depth", 0, 0, axis_index_groups=rings, tiled=True)


def to_other_core(value, source):
    pairs = [(device(x, z, source), device(x, z, 1 - source)) for x in ring for z in ring]
    return lax.ppermute(value, "depth", pairs)


def hop(value, source, target):
    return lax.ppermute(value, "depth", [(device(source, z, 0), device(target, z, 0)) for z in ring])


def body(object_slices, probe_wave, amplitudes, positions, counts):
    depth = lax.axis_index("depth")
    stripe = lax.axis_index("stripe")
    stage = depth // GROUP
    slot = (depth % GROUP) // 2
    core = depth % 2
    dft, chirp, pick = (jnp.asarray(t) for t in make_tables())
    place = lax.dynamic_slice_in_dim(positions, stripe * CAP, CAP, 0)
    live = lax.dynamic_slice_in_dim(counts, stripe, 1, 0)
    works = (core == 0) & (slot < live[0])

    def flag_of(t):
        return (works & (stage == t)).astype(jnp.int32)[None]

    own_re, own_im = object_slices[0, 0], object_slices[0, 1]
    back = [(i, (i - 1) % 4) for i in ring]
    after_re = lax.ppermute(own_re, "stripe", back)
    after_im = lax.ppermute(own_im, "stripe", back)
    even_re = exchange(cut_windows(place, own_re, after_re))
    even_im = exchange(cut_windows(place, own_im, after_im))
    odd_re, odd_im = to_other_core(even_re, 1), to_other_core(even_im, 1)
    wins = (even_re, even_im, odd_re, odd_im)

    pattern = lax.dynamic_index_in_dim(amplitudes, slot, 0, keepdims=False)
    wave, waves = probe_wave, None
    for t in range(STAGES - 1):
        wave, waves = forward_stage(flag_of(t), wave, wins, chirp, waves)
        wave = hop(wave, t, t + 1)
    wave, grads = turn_stage(flag_of(STAGES - 1), wave, wins, chirp, dft, pattern, pick)
    for t in reversed(range(STAGES - 1)):
        wave = hop(wave, t + 1, t)
        wave, grads = backward_stage(flag_of(t), wave, wins, chirp, waves, grads)

    forth = [(i, (i + 1) % 4) for i in ring]
    parts = []
    for even, odd in grads:
        odd = to_other_core(odd, 0)
        top, low = add_windows(place, live, exchange(jnp.where(core == 0, even, odd)))
        parts += [top, lax.ppermute(low, "stripe", forth)]
    return join(parts)


def solution(mesh):
    return jax.shard_map(
        body,
        mesh=mesh,
        in_specs=(P("depth", None, "stripe", None), P(), P("stripe", None, None), P(), P()),
        out_specs=P("depth", None, "stripe", None),
        check_vma=False,
    )
```

```python
import numpy as np

import jax
import jax.numpy as jnp
from jax import lax
from jax.experimental import pallas as pl
from jax.experimental.pallas import tpu as pltpu
from jax.sharding import PartitionSpec as P

WIN = 256
HALF = 128
ROWS = 256
COLS = 384
CAP = 4
GROUP = 8
STAGES = 4
CHUNK = 128
smoothing = 0.25
f32 = jnp.float32
bf16 = jnp.bfloat16


def split_np(table):
    high = table.astype(bf16)
    low = (table - high.astype(np.float64)).astype(bf16)
    return high, low


def make_tables():
    n = np.arange(HALF)[:, None]
    k = np.arange(HALF)[None, :]
    tables = []
    for parity in (0, 1):
        angle = -2.0 * np.pi * ((n * (2 * k + parity)) % WIN) / WIN
        c, s = np.cos(angle) / 16.0, np.sin(angle) / 16.0
        full = np.block([[c, s], [-s, c]])
        for table in (full, full.T):
            tables.extend(split_np(table))
    dft = np.stack(tables)
    freq = (((np.arange(WIN) + HALF) % WIN) - HALF).astype(np.float64)
    response = np.fft.ifft(np.exp(-1j * np.pi * freq**2 / (2.0 * WIN)))
    near = response[(n - k) % WIN]
    far = response[(n - k - HALF) % WIN]
    tables = []
    for block in ((near + far) / 2.0, (near - far) / 2.0):
        tables.extend(split_np(np.block([[block.real, block.imag], [-block.imag, block.real]])))
    chirp = np.stack(tables)
    order = np.concatenate([np.arange(0, WIN, 2), np.arange(1, WIN, 2)])
    pick = np.zeros((WIN, WIN))
    pick[np.arange(WIN), order] = 1.0
    return dft, chirp, np.stack([pick, pick.T]).astype(bf16)


SUM, DIFF = 0, 2
EVEN, EVEN_T, ODD, ODD_T = 0, 2, 4, 6


def halves(value):
    high = value.astype(bf16)
    low = (value - high.astype(f32)).astype(bf16)
    return high, low


def mm(a, b):
    return jnp.dot(a, b, preferred_element_type=f32)


def right_mul(data, dft, which):
    high, low = halves(data)
    return mm(high, dft[which]) + mm(low, dft[which]) + mm(high, dft[which + 1])


def left_mul(dft, which, data):
    high, low = halves(data)
    return mm(dft[which], high) + mm(dft[which], low) + mm(dft[which + 1], high)


def lanes(a, b):
    return jnp.concatenate([a, b], axis=1)


def rows(a, b):
    return jnp.concatenate([a, b], axis=0)


def propagate(source, sink, chirp):
    top, low = slice(0, HALF), slice(HALF, WIN)
    re_top, im_top = source(top)
    re_low, im_low = source(low)

    sr, si, dr, di = re_top + re_low, im_top + im_low, re_top - re_low, im_top - im_low
    re, im = rows(sr, dr), rows(si, di)
    scol = right_mul(lanes(re[:, :HALF] + re[:, HALF:], im[:, :HALF] + im[:, HALF:]), chirp, SUM)
    dcol = right_mul(lanes(re[:, :HALF] - re[:, HALF:], im[:, :HALF] - im[:, HALF:]), chirp, DIFF)
    im, re = lanes(scol[:, HALF:], dcol[:, HALF:]), lanes(scol[:, :HALF], dcol[:, :HALF])
    total = left_mul(chirp, SUM, rows(im[:HALF], re[:HALF]))
    diff = left_mul(chirp, DIFF, rows(im[HALF:], re[HALF:]))
    for part, both in ((top, total + diff), (low, total - diff)):
        im, re = both[:HALF], both[HALF:]
        sink(
            part,
            lanes(re[:, :HALF] + re[:, HALF:], re[:, :HALF] - re[:, HALF:]),
            lanes(im[:, :HALF] + im[:, HALF:], im[:, :HALF] - im[:, HALF:]),
        )


def exit_wave(source, sink, dft, mid, pointwise):
    for start in range(0, WIN, CHUNK):
        part = slice(start, start + CHUNK)
        re, im = source(part)
        even = lanes(re[:, :HALF] + re[:, HALF:], im[:, :HALF] + im[:, HALF:])
        odd = lanes(re[:, :HALF] - re[:, HALF:], im[:, :HALF] - im[:, HALF:])
        even = right_mul(even, dft, EVEN)
        odd = right_mul(odd, dft, ODD)
        mid[0, part, :] = lanes(even[:, :HALF], odd[:, :HALF])
        mid[1, part, :] = lanes(even[:, HALF:], odd[:, HALF:])
    re_top, re_low = mid[0, :HALF, :], mid[0, HALF:, :]
    im_top, im_low = mid[1, :HALF, :], mid[1, HALF:, :]
    even = left_mul(dft, EVEN_T, rows(re_top + re_low, im_top + im_low))
    odd = left_mul(dft, ODD_T, rows(re_top - re_low, im_top - im_low))
    even = pointwise(slice(0, HALF), even[:HALF], even[HALF:])
    odd = pointwise(slice(HALF, WIN), odd[:HALF], odd[HALF:])
    even = left_mul(dft, EVEN, rows(*even))
    odd = left_mul(dft, ODD, rows(*odd))
    mid[0, :HALF, :] = even[:HALF] + odd[:HALF]
    mid[0, HALF:, :] = even[:HALF] - odd[:HALF]
    mid[1, :HALF, :] = even[HALF:] + odd[HALF:]
    mid[1, HALF:, :] = even[HALF:] - odd[HALF:]
    for start in range(0, WIN, CHUNK):
        part = slice(start, start + CHUNK)
        re, im = mid[0, part, :], mid[1, part, :]
        even = right_mul(lanes(re[:, :HALF], im[:, :HALF]), dft, EVEN_T)
        odd = right_mul(lanes(re[:, HALF:], im[:, HALF:]), dft, ODD_T)
        total, diff = even + odd, even - odd
        sink(part, lanes(total[:, :HALF], diff[:, :HALF]), lanes(total[:, HALF:], diff[:, HALF:]))


CODED = WIN + 16
i16 = jnp.int16


def exponent(most):
    return jnp.ceil(jnp.log2(jnp.maximum(most, 1e-30)))


def encode(dst, part, value):
    exp = exponent(jnp.max(jnp.abs(value), axis=0, keepdims=True))
    scaled = jnp.round(value * (jnp.exp2(-exp) * 32767.0))
    dst[part, :] = scaled.astype(jnp.int32).astype(i16)
    return jnp.broadcast_to(exp, (8, value.shape[1])).astype(jnp.int32)


def encode_tail(dst, top, low):
    dst[WIN:, :] = jnp.concatenate([top, low], axis=0).astype(i16)


def decode(src, part):
    tail = src[WIN:, :].astype(jnp.int32)[8 * (part.start // HALF):][:1].astype(f32)
    return src[part, :].astype(jnp.int32).astype(f32) * (jnp.exp2(tail) * (1.0 / 32767.0))


TOP, LOW = slice(0, HALF), slice(HALF, WIN)


def encode_plane(dst, top, low):
    encode_tail(dst, encode(dst, TOP, top), encode(dst, LOW, low))


def decode_wave(dst, src):
    for comp in range(2):
        for part in (TOP, LOW):
            dst[comp, part, :] = decode(src.at[comp], part)


def encode_wave(dst, src):
    for comp in range(2):
        encode_plane(dst.at[comp], src[comp, TOP, :], src[comp, LOW, :])


def times(re, im, win, part):
    tr, ti = win[0, part, :], win[1, part, :]
    return re * tr - im * ti, re * ti + im * tr


class Ahead:
    def __init__(self, arrays, buf, sem, depth):
        self.arrays, self.buf, self.sem, self.depth = arrays, buf, sem, depth

    def copy(self, i):
        slot = i & (self.depth - 1)
        return pltpu.make_async_copy(self.arrays.at[i], self.buf.at[slot], self.sem.at[slot])

    def start(self, i):
        self.copy(i).start()

    def wait(self, i):
        self.copy(i).wait()

    def at(self, i):
        return self.buf.at[i & (self.depth - 1)]


class Fetch:
    def __init__(self, pairs, sem):
        self.copies = [pltpu.make_async_copy(src, dst, sem.at[i]) for i, (src, dst) in enumerate(pairs)]

    def start(self):
        for copy in self.copies:
            copy.start()

    def wait(self):
        for copy in self.copies:
            copy.wait()


def forward_slice(src, dst, windows, i, chirp):
    def source(part):
        return times(src[0, part, :], src[1, part, :], windows.at(i), part)

    def sink(part, re, im):
        dst[0, part, :] = re
        dst[1, part, :] = im

    propagate(source, sink, chirp)


def retreat(i, part, re, im, adj, wave, windows, grad, tails):
    wr, wi = wave[0, part, :], wave[1, part, :]
    half = part.start // HALF
    for comp, value in enumerate((wr * re - wi * im, -(wr * im + wi * re))):
        tails[comp, 8 * half:8 * half + 8, :] = encode(grad.at[comp], part, value)
    adj[0, part, :], adj[1, part, :] = times(re, im, windows.at(i), part)


def finish_grad(grad, tails):
    for comp in range(2):
        grad[comp, WIN:, :] = tails[comp].astype(i16)


def backward_slice(i, adj, wave, windows, chirp, grad, tails):
    def source(part):
        return adj[0, part, :], adj[1, part, :]

    def sink(part, re, im):
        retreat(i, part, re, im, adj, wave, windows, grad, tails)

    propagate(source, sink, chirp)
    finish_grad(grad, tails)


def copy_wave(dst, src):
    for comp in range(2):
        dst[comp] = src[comp].astype(f32)


def forward_kernel(first, flag, coded, wins, chirp, *rest):
    wave_out, waves, win_buf, win_sem, buf, sem = rest[-6:]
    windows = Ahead(wins, win_buf, win_sem, win_buf.shape[0])

    def store(i):
        slot = lax.rem(i, 3)
        return pltpu.make_async_copy(buf.at[slot], waves.at[i], sem.at[slot])

    @pl.when(flag[0] >= 4)
    def _():
        for i in range(DEPTH - 1):
            windows.start(jnp.int32(i))
        if first:
            copy_wave(buf.at[0], coded)
        else:
            decode_wave(buf.at[0], coded)

        @pl.loop(0, GROUP)
        def _(i):
            @pl.when(i + DEPTH - 1 < GROUP)
            def _():
                windows.start(i + DEPTH - 1)

            store(i).start()

            @pl.when(i >= 2)
            def _():
                store(i - 2).wait()

            windows.wait(i)
            forward_slice(buf.at[lax.rem(i, 3)], buf.at[lax.rem(i + 1, 3)], windows, i, chirp)

        encode_wave(wave_out, buf.at[GROUP % 3])
        store(jnp.int32(GROUP - 2)).wait()
        store(jnp.int32(GROUP - 1)).wait()


class Gradients:
    def __init__(self, grads, buf, sem):
        self.grads, self.buf, self.sem = grads, buf, sem

    def copy(self, i, odd):
        return pltpu.make_async_copy(self.buf.at[odd], self.grads[odd].at[i >> 1], self.sem.at[odd])

    def start(self, i):
        for odd in range(2):
            @pl.when((i & 1) == odd)
            def _():
                self.copy(i, odd).start()

    def wait(self, i):
        for odd in range(2):
            @pl.when((i & 1) == odd)
            def _():
                self.copy(i, odd).wait()


def turn_kernel(flag, coded, wins, chirp, dft_in, patterns, pick_in, adj_out, *rest):
    *grads, win_buf, win_sem, grad_buf, grad_sem, adj, tails = rest[:8]
    waves, mid, far_amp, dft, pattern, pick, late_sem = rest[8:]
    windows = Ahead(wins, win_buf, win_sem, win_buf.shape[0])
    out = Gradients(grads, grad_buf, grad_sem)
    end = GROUP - 1

    @pl.when(flag[0] >= 4)
    def _():
        for i in range(GROUP):
            windows.start(jnp.int32(i))
        late = Fetch([(dft_in, dft), (patterns.at[flag[0] & 3], pattern), (pick_in, pick)], late_sem)
        late.start()
        decode_wave(waves.at[0], coded)

        @pl.loop(0, end)
        def _(i):
            windows.wait(i)
            forward_slice(waves.at[i], waves.at[i + 1], windows, i, chirp)

        windows.wait(jnp.int32(end))
        late.wait()
        picked = mm(pick[0], pattern[...]).astype(bf16)
        far_amp[...] = mm(picked, pick[1])

        def source(part):
            return times(waves[end, 0, part, :], waves[end, 1, part, :], win_buf.at[end], part)

        def exit_point(part, re, im):
            smooth = jnp.sqrt(re * re + im * im + smoothing)
            factor = 1.0 - far_amp[part, :] / smooth
            return factor * re, factor * im

        def sink(part, re, im):
            retreat(end, part, re, -im, adj, waves.at[end], windows, grad_buf.at[end & 1], tails)

        exit_wave(source, sink, dft, mid, exit_point)
        finish_grad(grad_buf.at[end & 1], tails)
        out.start(jnp.int32(end))

        @pl.loop(0, end)
        def _(step):
            i = end - 1 - step

            @pl.when(step > 0)
            def _():
                out.wait(i + 2)

            backward_slice(i, adj, waves.at[i], windows, chirp, grad_buf.at[i & 1], tails)
            out.start(i)

        encode_wave(adj_out, adj)
        out.wait(jnp.int32(1))
        out.wait(jnp.int32(0))


def backward_kernel(final, flag, coded, wins, chirp, waves, *rest):
    rest = rest[2:]
    if not final:
        adj_out, rest = rest[0], rest[1:]
    *grads, win_buf, win_sem, grad_buf, grad_sem, adj, tails = rest[:8]
    wave_buf, wave_sem = rest[8:]
    windows = Ahead(wins, win_buf, win_sem, win_buf.shape[0])
    out = Gradients(grads, grad_buf, grad_sem)

    kept = Ahead(waves, wave_buf, wave_sem, wave_buf.shape[0])

    @pl.when(flag[0] >= 4)
    def _():
        for i in range(DEPTH - 1):
            windows.start(jnp.int32(GROUP - 1 - i))
            kept.start(jnp.int32(GROUP - 1 - i))
        decode_wave(adj, coded)

        @pl.loop(0, GROUP)
        def _(step):
            i = GROUP - 1 - step
            windows.wait(i)
            kept.wait(i)

            @pl.when(i >= DEPTH - 1)
            def _():
                windows.start(i - DEPTH + 1)
                kept.start(i - DEPTH + 1)

            @pl.when(step >= 2)
            def _():
                out.wait(i + 2)

            backward_slice(i, adj, kept.at(i), windows, chirp, grad_buf.at[i & 1], tails)
            out.start(i)

        if not final:
            encode_wave(adj_out, adj)
        out.wait(jnp.int32(1))
        out.wait(jnp.int32(0))


vmem = pl.BlockSpec(memory_space=pltpu.VMEM)
smem = pl.BlockSpec(memory_space=pltpu.SMEM)
hbm = pl.BlockSpec(memory_space=pltpu.HBM)
params = pltpu.CompilerParams(vmem_limit_bytes=24 * 2**20)
wave_shape = jax.ShapeDtypeStruct((2, CODED, WIN), i16)
waves_shape = pltpu.HBM((GROUP, 2, WIN, WIN), f32)
grads_shape = [pltpu.HBM((GROUP // 2, 2, CODED, WIN), i16)] * 2
dma = pltpu.SemaphoreType.DMA
DEPTH = 4
win_scratch = lambda depth: [pltpu.VMEM((depth, 2, WIN, WIN), f32), dma((depth,))]
grad_scratch = lambda: [
    pltpu.VMEM((2, 2, CODED, WIN), i16),
    dma((2,)),
    pltpu.VMEM((2, WIN, WIN), f32),
    pltpu.VMEM((2, 16, WIN), jnp.int32),
]


def in_hbm(value):
    return pltpu.with_memory_space_constraint(value, pltpu.HBM)


def forward_stage(flag, wave, wins, chirp, waves):
    first = waves is None
    args = [flag, wave, in_hbm(wins), chirp]
    args += [] if first else [in_hbm(waves)]
    return pl.pallas_call(
        lambda *refs: forward_kernel(first, *refs),
        in_specs=[smem, vmem, hbm, vmem] + [hbm] * (len(args) - 4),
        out_specs=[vmem, hbm],
        out_shape=[wave_shape, waves_shape],
        input_output_aliases={} if first else {4: 1},
        scratch_shapes=win_scratch(DEPTH) + [
            pltpu.VMEM((3, 2, WIN, WIN), f32),
            dma((3,)),
        ],
        compiler_params=params,
        name="forward_stage",
    )(*args)


def turn_stage(flag, wave, wins, chirp, dft, patterns, pick):
    return pl.pallas_call(
        turn_kernel,
        in_specs=[smem, vmem, hbm, vmem] + [hbm] * 3,
        out_specs=[vmem] + [hbm] * 2,
        out_shape=[wave_shape, *grads_shape],
        scratch_shapes=win_scratch(GROUP) + grad_scratch() + [
            pltpu.VMEM((GROUP, 2, WIN, WIN), f32),
            pltpu.VMEM((2, WIN, WIN), f32),
            pltpu.VMEM((WIN, WIN), f32),
            pltpu.VMEM((8, WIN, WIN), bf16),
            pltpu.VMEM((WIN, WIN), bf16),
            pltpu.VMEM((2, WIN, WIN), bf16),
            dma((3,)),
        ],
        compiler_params=params,
        name="turn_stage",
    )(flag, wave, in_hbm(wins), chirp, in_hbm(dft), in_hbm(patterns), in_hbm(pick))


def backward_stage(final, flag, adj, wins, chirp, waves, grads):
    lead = 0 if final else 1
    return pl.pallas_call(
        lambda *refs: backward_kernel(final, *refs),
        in_specs=[smem, vmem, hbm, vmem] + [hbm] * 3,
        out_specs=[vmem] * lead + [hbm] * 2,
        out_shape=[wave_shape] * lead + grads_shape,
        input_output_aliases={5 + k: lead + k for k in range(2)},
        scratch_shapes=win_scratch(DEPTH) + grad_scratch() + [
            pltpu.VMEM((DEPTH, 2, WIN, WIN), f32),
            dma((DEPTH,)),
        ],
        compiler_params=params,
        name="backward_stage",
    )(flag, adj, in_hbm(wins), chirp, in_hbm(waves), *[in_hbm(grad) for grad in grads])


FINE = 2.0**23


def pack_kernel(own, out):
    for start in range(0, ROWS, 64):
        part = slice(start, start + 64)
        words = [
            jnp.minimum(jnp.round(own[0, comp, part, :] * FINE).astype(jnp.int32), 2**23 - 1) for comp in range(2)
        ]
        both = ((words[0] & 255) << 8) + (words[1] & 255) - 2**15
        for plane, value in enumerate((both, words[0] >> 8, words[1] >> 8)):
            out[plane, part, :] = value.astype(i16)


def pack(own):
    return pl.pallas_call(
        pack_kernel,
        in_specs=[vmem],
        out_specs=vmem,
        out_shape=jax.ShapeDtypeStruct((3, ROWS, COLS), i16),
        compiler_params=params,
        name="pack",
    )(own)


def unpack_kernel(even, odd, out, buf, sem):
    copies = []
    for i in range(GROUP):
        array = (even, odd)[i % 2]
        for start in range(0, WIN, 64):
            part = slice(start, start + 64)
            both = array[i // 2, 0, part, :].astype(jnp.int32) + 2**15
            for comp, byte in enumerate((both >> 8, both & 255)):
                word = (array[i // 2, 1 + comp, part, :].astype(jnp.int32) << 8) + byte
                buf[i, comp, part, :] = word.astype(f32) * (1.0 / FINE)
        copies.append(pltpu.make_async_copy(buf.at[i], out.at[i], sem.at[i]))
        copies[-1].start()
    for copy in copies:
        copy.wait()


def unpack(even, odd):
    return pl.pallas_call(
        unpack_kernel,
        in_specs=[vmem] * 2,
        out_specs=hbm,
        out_shape=pltpu.HBM((GROUP, 2, WIN, WIN), f32),
        scratch_shapes=[pltpu.VMEM((GROUP, 2, WIN, WIN), f32), dma((GROUP,))],
        compiler_params=params,
        name="unpack",
    )(even, odd)


def corner(place, slot):
    row, col = place[slot, 0], place[slot, 1]
    base = pl.multiple_of((row >> 3) << 3, 8)
    return base, row - base, col


def cut_kernel(place, own, after, out, slab):
    for plane in range(3):
        slab[:ROWS, :] = own[plane].astype(jnp.int32)
        slab[ROWS:, :] = after[plane].astype(jnp.int32)
        for slot in range(CAP):
            base, shift, col = corner(place, slot)
            picked = slab[pl.ds(base, WIN + 8), :]
            picked = pltpu.roll(picked, lax.rem(COLS - col, COLS), 1)[:, :WIN]
            picked = pltpu.roll(picked, lax.rem(WIN + 8 - shift, WIN + 8), 0)[:WIN]
            out[slot, plane] = picked.astype(i16)


def cut_windows(place, own, after):
    return pl.pallas_call(
        cut_kernel,
        in_specs=[smem, vmem, vmem],
        out_specs=vmem,
        out_shape=jax.ShapeDtypeStruct((CAP, 3, WIN, WIN), i16),
        scratch_shapes=[pltpu.VMEM((2 * ROWS, COLS), jnp.int32)],
        compiler_params=params,
        name="cut_windows",
    )(place, own, after)


def add_kernel(place, live, grads, top, low, slab):
    slab[...] = jnp.zeros_like(slab)
    for slot in range(CAP):
        base, shift, col = corner(place, slot)

        @pl.when(slot < live[0])
        def _():
            for comp in range(2):
                own = grads.at[slot, comp]
                tall = jnp.concatenate([decode(own, TOP), decode(own, LOW), jnp.zeros((8, WIN), f32)], axis=0)
                tall = pltpu.roll(tall, shift, 0)
                wide = lanes(tall, jnp.zeros((WIN + 8, COLS - WIN), f32))
                slab[comp, pl.ds(base, WIN + 8), :] += pltpu.roll(wide, col, 1)
    for comp in range(2):
        top[comp] = slab[comp, :ROWS, :]
        encode_plane(low.at[comp], slab[comp, ROWS:ROWS + HALF, :], slab[comp, ROWS + HALF:, :])


def add_windows(place, live, grads):
    return pl.pallas_call(
        add_kernel,
        in_specs=[smem, smem, vmem],
        out_specs=[vmem, vmem],
        out_shape=[
            jax.ShapeDtypeStruct((2, ROWS, COLS), f32),
            jax.ShapeDtypeStruct((2, CODED, COLS), i16),
        ],
        scratch_shapes=[pltpu.VMEM((2, 2 * ROWS, COLS), f32)],
        compiler_params=params,
        name="add_windows",
    )(place, live, grads)


def pick_kernel(core, odd, even, out, sem):
    del even

    @pl.when(core[0] == 1)
    def _():
        copies = [pltpu.make_async_copy(odd.at[i, comp], out.at[i, comp], sem.at[2 * i + comp]) for i in range(4) for comp in range(2)]
        for copy in copies:
            copy.start()
        for copy in copies:
            copy.wait()


def pick_pile(core, even, odd):
    return pl.pallas_call(
        pick_kernel,
        in_specs=[smem, hbm, hbm],
        out_specs=hbm,
        out_shape=grads_shape[0],
        input_output_aliases={2: 0},
        scratch_shapes=[dma((8,))],
        compiler_params=params,
        name="pick_pile",
    )(core, odd, even)


def join_kernel(top, low, out):
    for comp in range(2):
        for part in (TOP, LOW):
            out[0, comp, part, :] = top[comp, part, :] + decode(low.at[comp], part)


def join(top, low):
    return pl.pallas_call(
        join_kernel,
        in_specs=[vmem] * 2,
        out_specs=vmem,
        out_shape=jax.ShapeDtypeStruct((1, 2, ROWS, COLS), f32),
        compiler_params=params,
        name="join",
    )(top, low)


def device(x, z, core):
    return x * GROUP + z * 2 + core


ring = range(4)
def ring_step(value, steps, source, target):
    pairs = [(device(x, z, source), device(x, (z + steps) % 4, target)) for x in ring for z in ring]
    return lax.ppermute(value, "depth", pairs)


rings = [[device(x, z, core) for z in ring] for x in ring for core in range(2)]


def exchange(value):
    return lax.all_to_all(value, "depth", 0, 0, axis_index_groups=rings, tiled=True)


def hop(value, source, target):
    return lax.ppermute(value, "depth", [(device(source, z, 0), device(target, z, 0)) for z in ring])


def body(object_slices, probe_wave, amplitudes, positions, counts):
    depth = lax.axis_index("depth")
    stripe = lax.axis_index("stripe")
    stage = depth // GROUP
    slot = (depth % GROUP) // 2
    core = depth % 2
    dft, chirp, pick = (jnp.asarray(t) for t in make_tables())
    place = lax.dynamic_slice_in_dim(positions, stripe * CAP, CAP, 0)
    live = lax.dynamic_slice_in_dim(counts, stripe, 1, 0)
    works = (core == 0) & (slot < live[0])

    def flag_of(t):
        return (slot + 4 * (works & (stage == t))).astype(jnp.int32)[None]

    own = pack(object_slices)
    after = lax.ppermute(own, "stripe", [(i, (i - 1) % 4) for i in ring])
    even = exchange(cut_windows(place, own, after))
    wins = unpack(even, ring_step(even, 0, 1, 0))

    wave, waves = probe_wave, None
    for t in range(STAGES - 1):
        wave, waves = forward_stage(flag_of(t), wave, wins, chirp, waves)
        wave = hop(wave, t, t + 1)
    wave, *grads = turn_stage(flag_of(STAGES - 1), wave, wins, chirp, dft, amplitudes, pick)
    for t in reversed(range(STAGES - 1)):
        wave = hop(wave, t + 1, t)
        results = backward_stage(t == 0, flag_of(t), wave, wins, chirp, waves, grads)
        grads = results[-2:]
        wave = results[0]

    pile = pick_pile(core.astype(jnp.int32)[None], grads[0], ring_step(grads[1], 0, 0, 1))
    top, low = add_windows(place, live, exchange(pile))
    return join(top, lax.ppermute(low, "stripe", [(i, (i + 1) % 4) for i in ring]))


def solution(mesh):
    return jax.shard_map(
        body,
        mesh=mesh,
        in_specs=(P("depth", None, "stripe", None), P(), P("stripe", None, None), P(), P()),
        out_specs=P("depth", None, "stripe", None),
        check_vma=False,
    )
```

```python
import numpy as np

import jax
import jax.numpy as jnp
from jax import lax
from jax.experimental import pallas as pl
from jax.experimental.pallas import tpu as pltpu
from jax.sharding import PartitionSpec as P

WIN = 256
HALF = 128
ROWS = 256
COLS = 384
CAP = 4
GROUP = 8
STAGES = 4
CHUNK = 128
smoothing = 0.25
f32 = jnp.float32
bf16 = jnp.bfloat16


def split_np(table):
    high = table.astype(bf16)
    low = (table - high.astype(np.float64)).astype(bf16)
    return high, low


def make_tables():
    n = np.arange(HALF)[:, None]
    k = np.arange(HALF)[None, :]
    tables = []
    for parity in (0, 1):
        angle = -2.0 * np.pi * ((n * (2 * k + parity)) % WIN) / WIN
        c, s = np.cos(angle) / 16.0, np.sin(angle) / 16.0
        full = np.block([[c, s], [-s, c]])
        for table in (full, full.T):
            tables.extend(split_np(table))
    dft = np.stack(tables)
    freq = (((np.arange(WIN) + HALF) % WIN) - HALF).astype(np.float64)
    response = np.fft.ifft(np.exp(-1j * np.pi * freq**2 / (2.0 * WIN)))
    near = response[(n - k) % WIN]
    far = response[(n - k - HALF) % WIN]
    tables = []
    for block in ((near + far) / 2.0, (near - far) / 2.0):
        tables.extend(split_np(np.block([[block.real, block.imag], [-block.imag, block.real]])))
    chirp = np.stack(tables)
    order = np.concatenate([np.arange(0, WIN, 2), np.arange(1, WIN, 2)])
    pick = np.zeros((WIN, WIN))
    pick[np.arange(WIN), order] = 1.0
    return dft, chirp, np.stack([pick, pick.T]).astype(bf16)


SUM, DIFF = 0, 2
EVEN, EVEN_T, ODD, ODD_T = 0, 2, 4, 6


def halves(value):
    high = value.astype(bf16)
    low = (value - high.astype(f32)).astype(bf16)
    return high, low


def mm(a, b):
    return jnp.dot(a, b, preferred_element_type=f32)


def right_mul(data, dft, which):
    high, low = halves(data)
    return mm(high, dft[which]) + mm(low, dft[which]) + mm(high, dft[which + 1])


def left_mul(dft, which, data):
    high, low = halves(data)
    return mm(dft[which], high) + mm(dft[which], low) + mm(dft[which + 1], high)


def lanes(a, b):
    return jnp.concatenate([a, b], axis=1)


def rows(a, b):
    return jnp.concatenate([a, b], axis=0)


def propagate(source, sink, chirp):
    top, low = slice(0, HALF), slice(HALF, WIN)
    re_top, im_top = source(top)
    re_low, im_low = source(low)

    sr, si, dr, di = re_top + re_low, im_top + im_low, re_top - re_low, im_top - im_low
    re, im = rows(sr, dr), rows(si, di)
    scol = right_mul(lanes(re[:, :HALF] + re[:, HALF:], im[:, :HALF] + im[:, HALF:]), chirp, SUM)
    dcol = right_mul(lanes(re[:, :HALF] - re[:, HALF:], im[:, :HALF] - im[:, HALF:]), chirp, DIFF)
    im, re = lanes(scol[:, HALF:], dcol[:, HALF:]), lanes(scol[:, :HALF], dcol[:, :HALF])
    total = left_mul(chirp, SUM, rows(im[:HALF], re[:HALF]))
    diff = left_mul(chirp, DIFF, rows(im[HALF:], re[HALF:]))
    for part, both in ((top, total + diff), (low, total - diff)):
        im, re = both[:HALF], both[HALF:]
        sink(
            part,
            lanes(re[:, :HALF] + re[:, HALF:], re[:, :HALF] - re[:, HALF:]),
            lanes(im[:, :HALF] + im[:, HALF:], im[:, :HALF] - im[:, HALF:]),
        )


def exit_wave(source, sink, dft, mid, pointwise):
    for start in range(0, WIN, CHUNK):
        part = slice(start, start + CHUNK)
        re, im = source(part)
        even = lanes(re[:, :HALF] + re[:, HALF:], im[:, :HALF] + im[:, HALF:])
        odd = lanes(re[:, :HALF] - re[:, HALF:], im[:, :HALF] - im[:, HALF:])
        even = right_mul(even, dft, EVEN)
        odd = right_mul(odd, dft, ODD)
        mid[0, part, :] = lanes(even[:, :HALF], odd[:, :HALF])
        mid[1, part, :] = lanes(even[:, HALF:], odd[:, HALF:])
    re_top, re_low = mid[0, :HALF, :], mid[0, HALF:, :]
    im_top, im_low = mid[1, :HALF, :], mid[1, HALF:, :]
    even = left_mul(dft, EVEN_T, rows(re_top + re_low, im_top + im_low))
    odd = left_mul(dft, ODD_T, rows(re_top - re_low, im_top - im_low))
    even = pointwise(slice(0, HALF), even[:HALF], even[HALF:])
    odd = pointwise(slice(HALF, WIN), odd[:HALF], odd[HALF:])
    even = left_mul(dft, EVEN, rows(*even))
    odd = left_mul(dft, ODD, rows(*odd))
    mid[0, :HALF, :] = even[:HALF] + odd[:HALF]
    mid[0, HALF:, :] = even[:HALF] - odd[:HALF]
    mid[1, :HALF, :] = even[HALF:] + odd[HALF:]
    mid[1, HALF:, :] = even[HALF:] - odd[HALF:]
    for start in range(0, WIN, CHUNK):
        part = slice(start, start + CHUNK)
        re, im = mid[0, part, :], mid[1, part, :]
        even = right_mul(lanes(re[:, :HALF], im[:, :HALF]), dft, EVEN_T)
        odd = right_mul(lanes(re[:, HALF:], im[:, HALF:]), dft, ODD_T)
        total, diff = even + odd, even - odd
        sink(part, lanes(total[:, :HALF], diff[:, :HALF]), lanes(total[:, HALF:], diff[:, HALF:]))


CODED = WIN + 16
i16 = jnp.int16


def exponent(most):
    return jnp.ceil(jnp.log2(jnp.maximum(most, 1e-30)))


def encode(dst, part, value):
    exp = exponent(jnp.max(jnp.abs(value), axis=0, keepdims=True))
    scaled = jnp.round(value * (jnp.exp2(-exp) * 32767.0))
    dst[part, :] = scaled.astype(jnp.int32).astype(i16)
    return jnp.broadcast_to(exp, (8, value.shape[1])).astype(jnp.int32)


def encode_tail(dst, top, low):
    dst[WIN:, :] = jnp.concatenate([top, low], axis=0).astype(i16)


def decode(src, part):
    tail = src[WIN:, :].astype(jnp.int32)[8 * (part.start // HALF):][:1].astype(f32)
    return src[part, :].astype(jnp.int32).astype(f32) * (jnp.exp2(tail) * (1.0 / 32767.0))


TOP, LOW = slice(0, HALF), slice(HALF, WIN)


def encode_plane(dst, top, low):
    encode_tail(dst, encode(dst, TOP, top), encode(dst, LOW, low))


def decode_wave(dst, src):
    for comp in range(2):
        for part in (TOP, LOW):
            dst[comp, part, :] = decode(src.at[comp], part)


def encode_wave(dst, src):
    for comp in range(2):
        encode_plane(dst.at[comp], src[comp, TOP, :], src[comp, LOW, :])


def times(re, im, win, part):
    tr, ti = win[0, part, :], win[1, part, :]
    return re * tr - im * ti, re * ti + im * tr


class Ahead:
    def __init__(self, arrays, buf, sem, depth):
        self.arrays, self.buf, self.sem, self.depth = arrays, buf, sem, depth

    def copy(self, i):
        slot = i & (self.depth - 1)
        return pltpu.make_async_copy(self.arrays.at[i], self.buf.at[slot], self.sem.at[slot])

    def start(self, i):
        self.copy(i).start()

    def wait(self, i):
        self.copy(i).wait()

    def at(self, i):
        return self.buf.at[i & (self.depth - 1)]


class Fetch:
    def __init__(self, pairs, sem):
        self.copies = [pltpu.make_async_copy(src, dst, sem.at[i]) for i, (src, dst) in enumerate(pairs)]

    def start(self):
        for copy in self.copies:
            copy.start()

    def wait(self):
        for copy in self.copies:
            copy.wait()


def forward_slice(src, dst, windows, i, chirp):
    def source(part):
        return times(src[0, part, :], src[1, part, :], windows.at(i), part)

    def sink(part, re, im):
        dst[0, part, :] = re
        dst[1, part, :] = im

    propagate(source, sink, chirp)


def retreat(i, part, re, im, adj, wave, windows, grad, tails):
    wr, wi = wave[0, part, :], wave[1, part, :]
    half = part.start // HALF
    for comp, value in enumerate((wr * re - wi * im, -(wr * im + wi * re))):
        if tails is None:
            grad[comp, part, :] = value
        else:
            tails[comp, 8 * half:8 * half + 8, :] = encode(grad.at[comp], part, value)
    adj[0, part, :], adj[1, part, :] = times(re, im, windows.at(i), part)


def finish_grad(grad, tails):
    for comp in range(2):
        grad[comp, WIN:, :] = tails[comp].astype(i16)


def backward_slice(i, adj, wave, windows, chirp, grad, tails):
    def source(part):
        return adj[0, part, :], adj[1, part, :]

    def sink(part, re, im):
        retreat(i, part, re, im, adj, wave, windows, grad, tails)

    propagate(source, sink, chirp)
    if tails is not None:
        finish_grad(grad, tails)


def copy_wave(dst, src):
    for comp in range(2):
        dst[comp] = src[comp].astype(f32)


def forward_kernel(first, flag, coded, wins, chirp, first_win, *rest):
    wave_out, waves, edge, win_buf, win_sem, buf, sem = rest[-7:]
    windows = Ahead(wins, win_buf, win_sem, win_buf.shape[0])

    def store(i):
        slot = lax.rem(i, 3)
        return pltpu.make_async_copy(buf.at[slot], waves.at[i], sem.at[slot])

    @pl.when(flag[0] >= 4)
    def _():
        for i in range(1, DEPTH - 1):
            windows.start(jnp.int32(i))
        copy_wave(win_buf.at[0], first_win)
        if first:
            copy_wave(buf.at[0], coded)
        else:
            decode_wave(buf.at[0], coded)

        @pl.loop(0, GROUP)
        def _(i):
            @pl.when(i + DEPTH - 1 < GROUP)
            def _():
                windows.start(i + DEPTH - 1)

            store(i).start()

            @pl.when(i >= 2)
            def _():
                store(i - 2).wait()

            @pl.when(i > 0)
            def _():
                windows.wait(i)

            forward_slice(buf.at[lax.rem(i, 3)], buf.at[lax.rem(i + 1, 3)], windows, i, chirp)

        encode_wave(wave_out, buf.at[GROUP % 3])
        copy_wave(edge, buf.at[(GROUP - 1) % 3])
        store(jnp.int32(GROUP - 2)).wait()
        store(jnp.int32(GROUP - 1)).wait()


class Gradients:
    def __init__(self, grads, buf, sem):
        self.grads, self.buf, self.sem = grads, buf, sem

    def copy(self, i, odd):
        return pltpu.make_async_copy(self.buf.at[odd], self.grads[odd].at[i >> 1], self.sem.at[odd])

    def start(self, i):
        for odd in range(2):
            @pl.when((i & 1) == odd)
            def _():
                self.copy(i, odd).start()

    def wait(self, i):
        for odd in range(2):
            @pl.when((i & 1) == odd)
            def _():
                self.copy(i, odd).wait()


def turn_kernel(flag, coded, wins, chirp, first_win, dft_in, patterns, pick_in, adj_out, *rest):
    *grads, win_buf, win_sem, grad_buf, grad_sem, adj = rest[:7]
    waves, mid, far_amp, dft, pattern, pick, late_sem = rest[7:]
    windows = Ahead(wins, win_buf, win_sem, win_buf.shape[0])
    out = Gradients(grads, grad_buf, grad_sem)
    end = GROUP - 1

    @pl.when(flag[0] >= 4)
    def _():
        for i in range(1, GROUP):
            windows.start(jnp.int32(i))
        copy_wave(win_buf.at[0], first_win)
        late = Fetch([(dft_in, dft), (patterns.at[flag[0] & 3], pattern), (pick_in, pick)], late_sem)
        late.start()
        decode_wave(waves.at[0], coded)

        @pl.loop(0, end)
        def _(i):
            @pl.when(i > 0)
            def _():
                windows.wait(i)

            forward_slice(waves.at[i], waves.at[i + 1], windows, i, chirp)

        windows.wait(jnp.int32(end))
        late.wait()
        picked = mm(pick[0], pattern[...]).astype(bf16)
        far_amp[...] = mm(picked, pick[1])

        def source(part):
            return times(waves[end, 0, part, :], waves[end, 1, part, :], win_buf.at[end], part)

        def exit_point(part, re, im):
            smooth = jnp.sqrt(re * re + im * im + smoothing)
            factor = 1.0 - far_amp[part, :] / smooth
            return factor * re, factor * im

        def sink(part, re, im):
            retreat(end, part, re, -im, adj, waves.at[end], windows, grad_buf.at[end & 1], None)

        exit_wave(source, sink, dft, mid, exit_point)
        out.start(jnp.int32(end))

        @pl.loop(0, end)
        def _(step):
            i = end - 1 - step

            @pl.when(step > 0)
            def _():
                out.wait(i + 2)

            backward_slice(i, adj, waves.at[i], windows, chirp, grad_buf.at[i & 1], None)
            out.start(i)

        encode_wave(adj_out, adj)
        out.wait(jnp.int32(1))
        out.wait(jnp.int32(0))


def backward_kernel(final, flag, coded, wins, chirp, waves, last_win, last_wave, *rest):
    rest = rest[2:]
    if not final:
        adj_out, rest = rest[0], rest[1:]
    *grads, win_buf, win_sem, grad_buf, grad_sem, adj, wave_buf, wave_sem = rest[:9]
    tails = rest[9] if final else None
    windows = Ahead(wins, win_buf, win_sem, win_buf.shape[0])
    out = Gradients(grads, grad_buf, grad_sem)

    kept = Ahead(waves, wave_buf, wave_sem, wave_buf.shape[0])

    @pl.when(flag[0] >= 4)
    def _():
        for i in range(1, DEPTH - 1):
            windows.start(jnp.int32(GROUP - 1 - i))
            kept.start(jnp.int32(GROUP - 1 - i))
        copy_wave(win_buf.at[(GROUP - 1) % DEPTH], last_win)
        copy_wave(wave_buf.at[(GROUP - 1) % DEPTH], last_wave)
        decode_wave(adj, coded)

        @pl.loop(0, GROUP)
        def _(step):
            i = GROUP - 1 - step
            @pl.when(step > 0)
            def _():
                windows.wait(i)
                kept.wait(i)

            @pl.when(i >= DEPTH - 1)
            def _():
                windows.start(i - DEPTH + 1)
                kept.start(i - DEPTH + 1)

            @pl.when(step >= 2)
            def _():
                out.wait(i + 2)

            backward_slice(i, adj, kept.at(i), windows, chirp, grad_buf.at[i & 1], tails)
            out.start(i)

        if not final:
            encode_wave(adj_out, adj)
        out.wait(jnp.int32(1))
        out.wait(jnp.int32(0))


vmem = pl.BlockSpec(memory_space=pltpu.VMEM)
smem = pl.BlockSpec(memory_space=pltpu.SMEM)
hbm = pl.BlockSpec(memory_space=pltpu.HBM)
params = pltpu.CompilerParams(vmem_limit_bytes=24 * 2**20)
wave_shape = jax.ShapeDtypeStruct((2, CODED, WIN), i16)
waves_shape = pltpu.HBM((GROUP, 2, WIN, WIN), f32)
grads_shape = [pltpu.HBM((GROUP // 2, 2, CODED, WIN), i16)] * 2
dma = pltpu.SemaphoreType.DMA
DEPTH = 4
win_scratch = lambda depth: [pltpu.VMEM((depth, 2, WIN, WIN), f32), dma((depth,))]
raw_shape = [pltpu.HBM((GROUP // 2, 2, WIN, WIN), f32)] * 2
grad_scratch = lambda coded: [
    pltpu.VMEM((2, 2, CODED, WIN), i16) if coded else pltpu.VMEM((2, 2, WIN, WIN), f32),
    dma((2,)),
    pltpu.VMEM((2, WIN, WIN), f32),
]
tail_scratch = lambda: [pltpu.VMEM((2, 16, WIN), jnp.int32)]


def in_hbm(value):
    return pltpu.with_memory_space_constraint(value, pltpu.HBM)


def forward_stage(flag, wave, wins, chirp, first_win, waves):
    first = waves is None
    args = [flag, wave, in_hbm(wins), chirp, first_win]
    args += [] if first else [in_hbm(waves)]
    return pl.pallas_call(
        lambda *refs: forward_kernel(first, *refs),
        in_specs=[smem, vmem, hbm, vmem, vmem] + [hbm] * (len(args) - 5),
        out_specs=[vmem, hbm, vmem],
        out_shape=[wave_shape, waves_shape, jax.ShapeDtypeStruct((2, WIN, WIN), f32)],
        input_output_aliases={} if first else {5: 1},
        scratch_shapes=win_scratch(DEPTH) + [
            pltpu.VMEM((3, 2, WIN, WIN), f32),
            dma((3,)),
        ],
        compiler_params=params,
        name="forward_stage",
    )(*args)


def turn_stage(flag, wave, wins, chirp, first_win, dft, patterns, pick):
    return pl.pallas_call(
        turn_kernel,
        in_specs=[smem, vmem, hbm, vmem, vmem] + [hbm] * 3,
        out_specs=[vmem] + [hbm] * 2,
        out_shape=[wave_shape, *raw_shape],
        scratch_shapes=win_scratch(GROUP) + grad_scratch(False) + [
            pltpu.VMEM((GROUP, 2, WIN, WIN), f32),
            pltpu.VMEM((2, WIN, WIN), f32),
            pltpu.VMEM((WIN, WIN), f32),
            pltpu.VMEM((8, WIN, WIN), bf16),
            pltpu.VMEM((WIN, WIN), bf16),
            pltpu.VMEM((2, WIN, WIN), bf16),
            dma((3,)),
        ],
        compiler_params=params,
        name="turn_stage",
    )(flag, wave, in_hbm(wins), chirp, first_win, in_hbm(dft), in_hbm(patterns), in_hbm(pick))


def backward_stage(final, flag, adj, wins, chirp, waves, last_win, last_wave, grads):
    lead = 0 if final else 1
    return pl.pallas_call(
        lambda *refs: backward_kernel(final, *refs),
        in_specs=[smem, vmem, hbm, vmem, hbm, vmem, vmem] + [hbm] * 2,
        out_specs=[vmem] * lead + [hbm] * 2,
        out_shape=[wave_shape] * lead + (grads_shape if final else raw_shape),
        input_output_aliases={7 + k: lead + k for k in range(2)},
        scratch_shapes=win_scratch(DEPTH) + grad_scratch(final) + [
            pltpu.VMEM((DEPTH, 2, WIN, WIN), f32),
            dma((DEPTH,)),
        ] + (tail_scratch() if final else []),
        compiler_params=params,
        name="backward_stage",
    )(flag, adj, in_hbm(wins), chirp, in_hbm(waves), last_win, last_wave, *[in_hbm(grad) for grad in grads])


def code_kernel(flag, even, odd, coded_even, coded_odd, buf, sem, out_buf, out_sem, tails):
    def load(i):
        return pltpu.make_async_copy((even, odd)[i % 2].at[i // 2], buf.at[i % DEPTH], sem.at[i % DEPTH])

    def store(i):
        return pltpu.make_async_copy(
            out_buf.at[i % 2], (coded_even, coded_odd)[i % 2].at[i // 2], out_sem.at[i % 2]
        )

    @pl.when(flag[0] >= 4)
    def _():
        for i in range(DEPTH):
            load(i).start()
        for i in range(GROUP):
            load(i).wait()
            if i >= 2:
                store(i - 2).wait()
            for comp in range(2):
                for half, part in enumerate((TOP, LOW)):
                    tails[comp, 8 * half:8 * half + 8, :] = encode(
                        out_buf.at[i % 2, comp], part, buf[i % DEPTH, comp, part, :]
                    )
            finish_grad(out_buf.at[i % 2], tails)
            store(i).start()
            if i + DEPTH < GROUP:
                load(i + DEPTH).start()
        store(GROUP - 2).wait()
        store(GROUP - 1).wait()


def code_grads(flag, grads):
    return pl.pallas_call(
        code_kernel,
        in_specs=[smem] + [hbm] * 2,
        out_specs=[hbm] * 2,
        out_shape=grads_shape,
        scratch_shapes=[
            pltpu.VMEM((DEPTH, 2, WIN, WIN), f32),
            dma((DEPTH,)),
            pltpu.VMEM((2, 2, CODED, WIN), i16),
            dma((2,)),
        ] + tail_scratch(),
        compiler_params=params,
        name="code_grads",
    )(flag, *[in_hbm(grad) for grad in grads])


FINE = 2.0**23


def pack_kernel(own, out):
    for start in range(0, ROWS, 64):
        part = slice(start, start + 64)
        words = [
            jnp.minimum(jnp.round(own[0, comp, part, :] * FINE).astype(jnp.int32), 2**23 - 1) for comp in range(2)
        ]
        both = ((words[0] & 255) << 8) + (words[1] & 255) - 2**15
        for plane, value in enumerate((both, words[0] >> 8, words[1] >> 8)):
            out[plane, part, :] = value.astype(i16)


def pack(own):
    return pl.pallas_call(
        pack_kernel,
        in_specs=[vmem],
        out_specs=vmem,
        out_shape=jax.ShapeDtypeStruct((3, ROWS, COLS), i16),
        compiler_params=params,
        name="pack",
    )(own)


def unpack_kernel(even, odd, out, first, last, buf, sem):
    copies = []
    for i in range(GROUP):
        array = (even, odd)[i % 2]
        for start in range(0, WIN, 64):
            part = slice(start, start + 64)
            both = array[i // 2, 0, part, :].astype(jnp.int32) + 2**15
            for comp, byte in enumerate((both >> 8, both & 255)):
                word = (array[i // 2, 1 + comp, part, :].astype(jnp.int32) << 8) + byte
                buf[i, comp, part, :] = word.astype(f32) * (1.0 / FINE)
                if i in (0, GROUP - 1):
                    (last if i else first)[comp, part, :] = buf[i, comp, part, :]
        copies.append(pltpu.make_async_copy(buf.at[i], out.at[i], sem.at[i]))
        copies[-1].start()
    for copy in copies:
        copy.wait()


def unpack(even, odd):
    return pl.pallas_call(
        unpack_kernel,
        in_specs=[vmem] * 2,
        out_specs=[hbm, vmem, vmem],
        out_shape=[pltpu.HBM((GROUP, 2, WIN, WIN), f32)] + [jax.ShapeDtypeStruct((2, WIN, WIN), f32)] * 2,
        scratch_shapes=[pltpu.VMEM((GROUP, 2, WIN, WIN), f32), dma((GROUP,))],
        compiler_params=params,
        name="unpack",
    )(even, odd)


def corner(place, slot):
    row, col = place[slot, 0], place[slot, 1]
    base = pl.multiple_of((row >> 3) << 3, 8)
    return base, row - base, col


def cut_kernel(place, own, after, out, slab):
    for plane in range(3):
        slab[:ROWS, :] = own[plane].astype(jnp.int32)
        slab[ROWS:, :] = after[plane].astype(jnp.int32)
        for slot in range(CAP):
            base, shift, col = corner(place, slot)
            picked = slab[pl.ds(base, WIN + 8), :]
            picked = pltpu.roll(picked, lax.rem(COLS - col, COLS), 1)[:, :WIN]
            picked = pltpu.roll(picked, lax.rem(WIN + 8 - shift, WIN + 8), 0)[:WIN]
            out[slot, plane] = picked.astype(i16)


def cut_windows(place, own, after):
    return pl.pallas_call(
        cut_kernel,
        in_specs=[smem, vmem, vmem],
        out_specs=vmem,
        out_shape=jax.ShapeDtypeStruct((CAP, 3, WIN, WIN), i16),
        scratch_shapes=[pltpu.VMEM((2 * ROWS, COLS), jnp.int32)],
        compiler_params=params,
        name="cut_windows",
    )(place, own, after)


def add_kernel(place, live, grads, top, low, slab):
    slab[...] = jnp.zeros_like(slab)
    for slot in range(CAP):
        base, shift, col = corner(place, slot)

        @pl.when(slot < live[0])
        def _():
            for comp in range(2):
                own = grads.at[slot, comp]
                tall = jnp.concatenate([decode(own, TOP), decode(own, LOW), jnp.zeros((8, WIN), f32)], axis=0)
                tall = pltpu.roll(tall, shift, 0)
                wide = lanes(tall, jnp.zeros((WIN + 8, COLS - WIN), f32))
                slab[comp, pl.ds(base, WIN + 8), :] += pltpu.roll(wide, col, 1)
    for comp in range(2):
        top[comp] = slab[comp, :ROWS, :]
        encode_plane(low.at[comp], slab[comp, ROWS:ROWS + HALF, :], slab[comp, ROWS + HALF:, :])


def add_windows(place, live, grads):
    return pl.pallas_call(
        add_kernel,
        in_specs=[smem, smem, vmem],
        out_specs=[vmem, vmem],
        out_shape=[
            jax.ShapeDtypeStruct((2, ROWS, COLS), f32),
            jax.ShapeDtypeStruct((2, CODED, COLS), i16),
        ],
        scratch_shapes=[pltpu.VMEM((2, 2 * ROWS, COLS), f32)],
        compiler_params=params,
        name="add_windows",
    )(place, live, grads)


def pick_kernel(core, odd, even, out, sem):
    del even

    @pl.when(core[0] == 1)
    def _():
        copies = [pltpu.make_async_copy(odd.at[i, comp], out.at[i, comp], sem.at[2 * i + comp]) for i in range(4) for comp in range(2)]
        for copy in copies:
            copy.start()
        for copy in copies:
            copy.wait()


def pick_pile(core, even, odd):
    return pl.pallas_call(
        pick_kernel,
        in_specs=[smem, hbm, hbm],
        out_specs=hbm,
        out_shape=grads_shape[0],
        input_output_aliases={2: 0},
        scratch_shapes=[dma((8,))],
        compiler_params=params,
        name="pick_pile",
    )(core, odd, even)


def join_kernel(top, low, out):
    for comp in range(2):
        for part in (TOP, LOW):
            out[0, comp, part, :] = top[comp, part, :] + decode(low.at[comp], part)


def join(top, low):
    return pl.pallas_call(
        join_kernel,
        in_specs=[vmem] * 2,
        out_specs=vmem,
        out_shape=jax.ShapeDtypeStruct((1, 2, ROWS, COLS), f32),
        compiler_params=params,
        name="join",
    )(top, low)


def device(x, z, core):
    return x * GROUP + z * 2 + core


ring = range(4)
def ring_step(value, steps, source, target):
    pairs = [(device(x, z, source), device(x, (z + steps) % 4, target)) for x in ring for z in ring]
    return lax.ppermute(value, "depth", pairs)


rings = [[device(x, z, core) for z in ring] for x in ring for core in range(2)]


def exchange(value):
    return lax.all_to_all(value, "depth", 0, 0, axis_index_groups=rings, tiled=True)


def hop(value, source, target):
    return lax.ppermute(value, "depth", [(device(source, z, 0), device(target, z, 0)) for z in ring])


def body(object_slices, probe_wave, amplitudes, positions, counts):
    depth = lax.axis_index("depth")
    stripe = lax.axis_index("stripe")
    stage = depth // GROUP
    slot = (depth % GROUP) // 2
    core = depth % 2
    dft, chirp, pick = (jnp.asarray(t) for t in make_tables())
    place = lax.dynamic_slice_in_dim(positions, stripe * CAP, CAP, 0)
    live = lax.dynamic_slice_in_dim(counts, stripe, 1, 0)
    works = (core == 0) & (slot < live[0])

    def flag_of(t):
        return (slot + 4 * (works & (stage == t))).astype(jnp.int32)[None]

    own = pack(object_slices)
    after = lax.ppermute(own, "stripe", [(i, (i - 1) % 4) for i in ring])
    even = exchange(cut_windows(place, own, after))
    wins, first, final_win = unpack(even, ring_step(even, 0, 1, 0))

    wave, waves, edges = probe_wave, None, []
    for t in range(STAGES - 1):
        wave, waves, edge = forward_stage(flag_of(t), wave, wins, chirp, first, waves)
        edges.append(edge)
        wave = hop(wave, t, t + 1)
    wave, *grads = turn_stage(flag_of(STAGES - 1), wave, wins, chirp, first, dft, amplitudes, pick)
    for t in reversed(range(STAGES - 1)):
        wave = hop(wave, t + 1, t)
        if t == 0:
            grads = code_grads((4 * (works & (stage > 0))).astype(jnp.int32)[None], grads)
        results = backward_stage(t == 0, flag_of(t), wave, wins, chirp, waves, final_win, edges[t], grads)
        grads = results[-2:]
        wave = results[0]

    pile = pick_pile(core.astype(jnp.int32)[None], grads[0], ring_step(grads[1], 0, 0, 1))
    top, low = add_windows(place, live, exchange(pile))
    return join(top, lax.ppermute(low, "stripe", [(i, (i + 1) % 4) for i in ring]))


def solution(mesh):
    return jax.shard_map(
        body,
        mesh=mesh,
        in_specs=(P("depth", None, "stripe", None), P(), P("stripe", None, None), P(), P()),
        out_specs=P("depth", None, "stripe", None),
        check_vma=False,
    )
```

```python
import numpy as np

import jax
import jax.numpy as jnp
from jax import lax
from jax.experimental import pallas as pl
from jax.experimental.pallas import tpu as pltpu
from jax.sharding import PartitionSpec as P

WIN = 256
HALF = 128
ROWS = 256
COLS = 384
CAP = 4
GROUP = 8
STAGES = 4
CHUNK = 128
smoothing = 0.25
f32 = jnp.float32
bf16 = jnp.bfloat16


def split_np(table):
    high = table.astype(bf16)
    low = (table - high.astype(np.float64)).astype(bf16)
    return high, low


def make_tables():
    n = np.arange(HALF)[:, None]
    k = np.arange(HALF)[None, :]
    tables = []
    for parity in (0, 1):
        angle = -2.0 * np.pi * ((n * (2 * k + parity)) % WIN) / WIN
        c, s = np.cos(angle) / 16.0, np.sin(angle) / 16.0
        full = np.block([[c, s], [-s, c]])
        for table in (full, full.T):
            tables.extend(split_np(table))
    dft = np.stack(tables)
    freq = (((np.arange(WIN) + HALF) % WIN) - HALF).astype(np.float64)
    response = np.fft.ifft(np.exp(-1j * np.pi * freq**2 / (2.0 * WIN)))
    near = response[(n - k) % WIN]
    far = response[(n - k - HALF) % WIN]
    tables = []
    for block in ((near + far) / 2.0, (near - far) / 2.0):
        tables.extend(split_np(np.block([[block.real, block.imag], [-block.imag, block.real]])))
    chirp = np.stack(tables)
    order = np.concatenate([np.arange(0, WIN, 2), np.arange(1, WIN, 2)])
    pick = np.zeros((WIN, WIN))
    pick[np.arange(WIN), order] = 1.0
    return dft, chirp, np.stack([pick, pick.T]).astype(bf16)


SUM, DIFF = 0, 2
EVEN, EVEN_T, ODD, ODD_T = 0, 2, 4, 6


def halves(value):
    high = value.astype(bf16)
    low = (value - high.astype(f32)).astype(bf16)
    return high, low


def mm(a, b):
    return jnp.dot(a, b, preferred_element_type=f32)


def right_mul(data, dft, which):
    high, low = halves(data)
    return mm(high, dft[which]) + mm(low, dft[which]) + mm(high, dft[which + 1])


def left_mul(dft, which, data):
    high, low = halves(data)
    return mm(dft[which], high) + mm(dft[which], low) + mm(dft[which + 1], high)


def lanes(a, b):
    return jnp.concatenate([a, b], axis=1)


def rows(a, b):
    return jnp.concatenate([a, b], axis=0)


def propagate(source, sink, chirp):
    top, low = slice(0, HALF), slice(HALF, WIN)
    re_top, im_top = source(top)
    re_low, im_low = source(low)

    sr, si, dr, di = re_top + re_low, im_top + im_low, re_top - re_low, im_top - im_low
    re, im = rows(sr, dr), rows(si, di)
    scol = right_mul(lanes(re[:, :HALF] + re[:, HALF:], im[:, :HALF] + im[:, HALF:]), chirp, SUM)
    dcol = right_mul(lanes(re[:, :HALF] - re[:, HALF:], im[:, :HALF] - im[:, HALF:]), chirp, DIFF)
    im, re = lanes(scol[:, HALF:], dcol[:, HALF:]), lanes(scol[:, :HALF], dcol[:, :HALF])
    total = left_mul(chirp, SUM, rows(im[:HALF], re[:HALF]))
    diff = left_mul(chirp, DIFF, rows(im[HALF:], re[HALF:]))
    for part, both in ((top, total + diff), (low, total - diff)):
        im, re = both[:HALF], both[HALF:]
        sink(
            part,
            lanes(re[:, :HALF] + re[:, HALF:], re[:, :HALF] - re[:, HALF:]),
            lanes(im[:, :HALF] + im[:, HALF:], im[:, :HALF] - im[:, HALF:]),
        )


def exit_wave(source, sink, dft, mid, pointwise):
    for start in range(0, WIN, CHUNK):
        part = slice(start, start + CHUNK)
        re, im = source(part)
        even = lanes(re[:, :HALF] + re[:, HALF:], im[:, :HALF] + im[:, HALF:])
        odd = lanes(re[:, :HALF] - re[:, HALF:], im[:, :HALF] - im[:, HALF:])
        even = right_mul(even, dft, EVEN)
        odd = right_mul(odd, dft, ODD)
        mid[0, part, :] = lanes(even[:, :HALF], odd[:, :HALF])
        mid[1, part, :] = lanes(even[:, HALF:], odd[:, HALF:])
    re_top, re_low = mid[0, :HALF, :], mid[0, HALF:, :]
    im_top, im_low = mid[1, :HALF, :], mid[1, HALF:, :]
    even = left_mul(dft, EVEN_T, rows(re_top + re_low, im_top + im_low))
    odd = left_mul(dft, ODD_T, rows(re_top - re_low, im_top - im_low))
    even = pointwise(slice(0, HALF), even[:HALF], even[HALF:])
    odd = pointwise(slice(HALF, WIN), odd[:HALF], odd[HALF:])
    even = left_mul(dft, EVEN, rows(*even))
    odd = left_mul(dft, ODD, rows(*odd))
    mid[0, :HALF, :] = even[:HALF] + odd[:HALF]
    mid[0, HALF:, :] = even[:HALF] - odd[:HALF]
    mid[1, :HALF, :] = even[HALF:] + odd[HALF:]
    mid[1, HALF:, :] = even[HALF:] - odd[HALF:]
    for start in range(0, WIN, CHUNK):
        part = slice(start, start + CHUNK)
        re, im = mid[0, part, :], mid[1, part, :]
        even = right_mul(lanes(re[:, :HALF], im[:, :HALF]), dft, EVEN_T)
        odd = right_mul(lanes(re[:, HALF:], im[:, HALF:]), dft, ODD_T)
        total, diff = even + odd, even - odd
        sink(part, lanes(total[:, :HALF], diff[:, :HALF]), lanes(total[:, HALF:], diff[:, HALF:]))


CODED = WIN + 16
i16 = jnp.int16


def exponent(most):
    return jnp.ceil(jnp.log2(jnp.maximum(most, 1e-30)))


def encode(dst, part, value):
    exp = exponent(jnp.max(jnp.abs(value), axis=0, keepdims=True))
    scaled = jnp.round(value * (jnp.exp2(-exp) * 32767.0))
    dst[part, :] = scaled.astype(jnp.int32).astype(i16)
    return jnp.broadcast_to(exp, (8, value.shape[1])).astype(jnp.int32)


def encode_tail(dst, top, low):
    dst[WIN:, :] = jnp.concatenate([top, low], axis=0).astype(i16)


def decode(src, part):
    tail = src[WIN:, :].astype(jnp.int32)[8 * (part.start // HALF):][:1].astype(f32)
    return src[part, :].astype(jnp.int32).astype(f32) * (jnp.exp2(tail) * (1.0 / 32767.0))


TOP, LOW = slice(0, HALF), slice(HALF, WIN)


def encode_plane(dst, top, low):
    encode_tail(dst, encode(dst, TOP, top), encode(dst, LOW, low))


def decode_wave(dst, src):
    for comp in range(2):
        for part in (TOP, LOW):
            dst[comp, part, :] = decode(src.at[comp], part)


def encode_wave(dst, src):
    for comp in range(2):
        encode_plane(dst.at[comp], src[comp, TOP, :], src[comp, LOW, :])


def times(re, im, win, part):
    tr, ti = win[0, part, :], win[1, part, :]
    return re * tr - im * ti, re * ti + im * tr


class Ahead:
    def __init__(self, arrays, buf, sem, depth):
        self.arrays, self.buf, self.sem, self.depth = arrays, buf, sem, depth

    def copy(self, i):
        slot = i & (self.depth - 1)
        return pltpu.make_async_copy(self.arrays.at[i], self.buf.at[slot], self.sem.at[slot])

    def start(self, i):
        self.copy(i).start()

    def wait(self, i):
        self.copy(i).wait()

    def at(self, i):
        return self.buf.at[i & (self.depth - 1)]


class Fetch:
    def __init__(self, pairs, sem):
        self.copies = [pltpu.make_async_copy(src, dst, sem.at[i]) for i, (src, dst) in enumerate(pairs)]

    def start(self):
        for copy in self.copies:
            copy.start()

    def wait(self):
        for copy in self.copies:
            copy.wait()


def forward_slice(src, dst, windows, i, chirp):
    def source(part):
        return times(src[0, part, :], src[1, part, :], windows.at(i), part)

    def sink(part, re, im):
        dst[0, part, :] = re
        dst[1, part, :] = im

    propagate(source, sink, chirp)


def retreat(i, part, re, im, adj, wave, windows, grad, tails):
    wr, wi = wave[0, part, :], wave[1, part, :]
    half = part.start // HALF
    for comp, value in enumerate((wr * re - wi * im, -(wr * im + wi * re))):
        if tails is None:
            grad[comp, part, :] = value
        else:
            tails[comp, 8 * half:8 * half + 8, :] = encode(grad.at[comp], part, value)
    adj[0, part, :], adj[1, part, :] = times(re, im, windows.at(i), part)


def finish_grad(grad, tails):
    for comp in range(2):
        grad[comp, WIN:, :] = tails[comp].astype(i16)


def backward_slice(i, adj, wave, windows, chirp, grad, tails):
    def source(part):
        return adj[0, part, :], adj[1, part, :]

    def sink(part, re, im):
        retreat(i, part, re, im, adj, wave, windows, grad, tails)

    propagate(source, sink, chirp)
    if tails is not None:
        finish_grad(grad, tails)


def copy_wave(dst, src):
    for comp in range(2):
        dst[comp] = src[comp].astype(f32)


def forward_kernel(first, flag, coded, wins, chirp, first_win, *rest):
    wave_out, waves, win_buf, win_sem, buf, sem = rest[-6:]
    windows = Ahead(wins, win_buf, win_sem, win_buf.shape[0])

    def store(i):
        slot = lax.rem(i, 3)
        return pltpu.make_async_copy(buf.at[slot], waves.at[i], sem.at[slot])

    @pl.when(flag[0] >= 4)
    def _():
        for i in range(1, DEPTH - 1):
            windows.start(jnp.int32(i))
        copy_wave(win_buf.at[0], first_win)
        if first:
            copy_wave(buf.at[0], coded)
        else:
            decode_wave(buf.at[0], coded)

        @pl.loop(0, GROUP)
        def _(i):
            @pl.when(i + DEPTH - 1 < GROUP)
            def _():
                windows.start(i + DEPTH - 1)

            store(i).start()

            @pl.when(i >= 2)
            def _():
                store(i - 2).wait()

            @pl.when(i > 0)
            def _():
                windows.wait(i)

            forward_slice(buf.at[lax.rem(i, 3)], buf.at[lax.rem(i + 1, 3)], windows, i, chirp)

        encode_wave(wave_out, buf.at[GROUP % 3])
        store(jnp.int32(GROUP - 2)).wait()
        store(jnp.int32(GROUP - 1)).wait()


class Gradients:
    def __init__(self, grads, buf, sem):
        self.grads, self.buf, self.sem = grads, buf, sem

    def copy(self, i, odd):
        return pltpu.make_async_copy(self.buf.at[odd], self.grads[odd].at[i >> 1], self.sem.at[odd])

    def start(self, i):
        for odd in range(2):
            @pl.when((i & 1) == odd)
            def _():
                self.copy(i, odd).start()

    def wait(self, i):
        for odd in range(2):
            @pl.when((i & 1) == odd)
            def _():
                self.copy(i, odd).wait()


def turn_kernel(flag, coded, wins, chirp, first_win, dft_in, patterns, pick_in, adj_out, *rest):
    *grads, win_buf, win_sem, grad_buf, grad_sem, adj = rest[:7]
    waves, mid, far_amp, dft, pattern, pick, late_sem = rest[7:]
    windows = Ahead(wins, win_buf, win_sem, win_buf.shape[0])
    out = Gradients(grads, grad_buf, grad_sem)
    end = GROUP - 1

    @pl.when(flag[0] >= 4)
    def _():
        for i in range(1, GROUP):
            windows.start(jnp.int32(i))
        copy_wave(win_buf.at[0], first_win)
        late = Fetch([(dft_in, dft), (patterns.at[flag[0] & 3], pattern), (pick_in, pick)], late_sem)
        late.start()
        decode_wave(waves.at[0], coded)

        @pl.loop(0, end)
        def _(i):
            @pl.when(i > 0)
            def _():
                windows.wait(i)

            forward_slice(waves.at[i], waves.at[i + 1], windows, i, chirp)

        windows.wait(jnp.int32(end))
        late.wait()
        picked = mm(pick[0], pattern[...]).astype(bf16)
        far_amp[...] = mm(picked, pick[1])

        def source(part):
            return times(waves[end, 0, part, :], waves[end, 1, part, :], win_buf.at[end], part)

        def exit_point(part, re, im):
            smooth = jnp.sqrt(re * re + im * im + smoothing)
            factor = 1.0 - far_amp[part, :] / smooth
            return factor * re, factor * im

        def sink(part, re, im):
            retreat(end, part, re, -im, adj, waves.at[end], windows, grad_buf.at[end & 1], None)

        exit_wave(source, sink, dft, mid, exit_point)
        out.start(jnp.int32(end))

        @pl.loop(0, end)
        def _(step):
            i = end - 1 - step

            @pl.when(step > 0)
            def _():
                out.wait(i + 2)

            backward_slice(i, adj, waves.at[i], windows, chirp, grad_buf.at[i & 1], None)
            out.start(i)

        encode_wave(adj_out, adj)
        out.wait(jnp.int32(1))
        out.wait(jnp.int32(0))


def backward_kernel(final, flag, coded, wins, chirp, waves, last_win, last_wave, *rest):
    rest = rest[2:]
    if not final:
        adj_out, rest = rest[0], rest[1:]
    *grads, win_buf, win_sem, grad_buf, grad_sem, adj, wave_buf, wave_sem = rest[:9]
    tails = rest[9] if final else None
    windows = Ahead(wins, win_buf, win_sem, win_buf.shape[0])
    out = Gradients(grads, grad_buf, grad_sem)

    kept = Ahead(waves, wave_buf, wave_sem, wave_buf.shape[0])

    @pl.when(flag[0] >= 4)
    def _():
        for i in range(1, DEPTH - 1):
            windows.start(jnp.int32(GROUP - 1 - i))
            kept.start(jnp.int32(GROUP - 1 - i))
        copy_wave(win_buf.at[(GROUP - 1) % DEPTH], last_win)
        copy_wave(wave_buf.at[(GROUP - 1) % DEPTH], last_wave)
        decode_wave(adj, coded)

        @pl.loop(0, GROUP)
        def _(step):
            i = GROUP - 1 - step
            @pl.when(step > 0)
            def _():
                windows.wait(i)
                kept.wait(i)

            @pl.when(i >= DEPTH - 1)
            def _():
                windows.start(i - DEPTH + 1)
                kept.start(i - DEPTH + 1)

            @pl.when(step >= 2)
            def _():
                out.wait(i + 2)

            backward_slice(i, adj, kept.at(i), windows, chirp, grad_buf.at[i & 1], tails)
            out.start(i)

        if not final:
            encode_wave(adj_out, adj)
        out.wait(jnp.int32(1))
        out.wait(jnp.int32(0))


vmem = pl.BlockSpec(memory_space=pltpu.VMEM)
smem = pl.BlockSpec(memory_space=pltpu.SMEM)
hbm = pl.BlockSpec(memory_space=pltpu.HBM)
params = pltpu.CompilerParams(vmem_limit_bytes=24 * 2**20)
wave_shape = jax.ShapeDtypeStruct((2, CODED, WIN), i16)
waves_shape = pltpu.HBM((GROUP, 2, WIN, WIN), f32)
grads_shape = [pltpu.HBM((GROUP // 2, 2, CODED, WIN), i16)] * 2
dma = pltpu.SemaphoreType.DMA
DEPTH = 4
win_scratch = lambda depth: [pltpu.VMEM((depth, 2, WIN, WIN), f32), dma((depth,))]
raw_shape = [pltpu.HBM((GROUP // 2, 2, WIN, WIN), f32)] * 2
grad_scratch = lambda coded: [
    pltpu.VMEM((2, 2, CODED, WIN), i16) if coded else pltpu.VMEM((2, 2, WIN, WIN), f32),
    dma((2,)),
    pltpu.VMEM((2, WIN, WIN), f32),
]
tail_scratch = lambda: [pltpu.VMEM((2, 16, WIN), jnp.int32)]


def in_hbm(value):
    return pltpu.with_memory_space_constraint(value, pltpu.HBM)


def forward_stage(flag, wave, wins, chirp, first_win, waves):
    first = waves is None
    args = [flag, wave, in_hbm(wins), chirp, first_win]
    args += [] if first else [in_hbm(waves)]
    return pl.pallas_call(
        lambda *refs: forward_kernel(first, *refs),
        in_specs=[smem, vmem, hbm, vmem, vmem] + [hbm] * (len(args) - 5),
        out_specs=[vmem, hbm],
        out_shape=[wave_shape, waves_shape],
        input_output_aliases={} if first else {5: 1},
        scratch_shapes=win_scratch(DEPTH) + [
            pltpu.VMEM((3, 2, WIN, WIN), f32),
            dma((3,)),
        ],
        compiler_params=params,
        name="forward_stage",
    )(*args)


def turn_stage(flag, wave, wins, chirp, first_win, dft, patterns, pick):
    return pl.pallas_call(
        turn_kernel,
        in_specs=[smem, vmem, hbm, vmem, vmem] + [hbm] * 3,
        out_specs=[vmem] + [hbm] * 2,
        out_shape=[wave_shape, *raw_shape],
        scratch_shapes=win_scratch(GROUP) + grad_scratch(False) + [
            pltpu.VMEM((GROUP, 2, WIN, WIN), f32),
            pltpu.VMEM((2, WIN, WIN), f32),
            pltpu.VMEM((WIN, WIN), f32),
            pltpu.VMEM((8, WIN, WIN), bf16),
            pltpu.VMEM((WIN, WIN), bf16),
            pltpu.VMEM((2, WIN, WIN), bf16),
            dma((3,)),
        ],
        compiler_params=params,
        name="turn_stage",
    )(flag, wave, in_hbm(wins), chirp, first_win, in_hbm(dft), in_hbm(patterns), in_hbm(pick))


def backward_stage(final, flag, adj, wins, chirp, waves, last_win, last_wave, grads):
    lead = 0 if final else 1
    return pl.pallas_call(
        lambda *refs: backward_kernel(final, *refs),
        in_specs=[smem, vmem, hbm, vmem, hbm, vmem, vmem] + [hbm] * 2,
        out_specs=[vmem] * lead + [hbm] * 2,
        out_shape=[wave_shape] * lead + (grads_shape if final else raw_shape),
        input_output_aliases={7 + k: lead + k for k in range(2)},
        scratch_shapes=win_scratch(DEPTH) + grad_scratch(final) + [
            pltpu.VMEM((DEPTH, 2, WIN, WIN), f32),
            dma((DEPTH,)),
        ] + (tail_scratch() if final else []),
        compiler_params=params,
        name="backward_stage",
    )(flag, adj, in_hbm(wins), chirp, in_hbm(waves), last_win, last_wave, *[in_hbm(grad) for grad in grads])


def code_kernel(flag, even, odd, coded_even, coded_odd, buf, sem, out_buf, out_sem, tails):
    def load(i):
        return pltpu.make_async_copy((even, odd)[i % 2].at[i // 2], buf.at[i % DEPTH], sem.at[i % DEPTH])

    def store(i):
        return pltpu.make_async_copy(
            out_buf.at[i % 2], (coded_even, coded_odd)[i % 2].at[i // 2], out_sem.at[i % 2]
        )

    @pl.when(flag[0] >= 4)
    def _():
        for i in range(DEPTH):
            load(i).start()
        for i in range(GROUP):
            load(i).wait()
            if i >= 2:
                store(i - 2).wait()
            for comp in range(2):
                for half, part in enumerate((TOP, LOW)):
                    tails[comp, 8 * half:8 * half + 8, :] = encode(
                        out_buf.at[i % 2, comp], part, buf[i % DEPTH, comp, part, :]
                    )
            finish_grad(out_buf.at[i % 2], tails)
            store(i).start()
            if i + DEPTH < GROUP:
                load(i + DEPTH).start()
        store(GROUP - 2).wait()
        store(GROUP - 1).wait()


def code_grads(flag, grads):
    return pl.pallas_call(
        code_kernel,
        in_specs=[smem] + [hbm] * 2,
        out_specs=[hbm] * 2,
        out_shape=grads_shape,
        scratch_shapes=[
            pltpu.VMEM((DEPTH, 2, WIN, WIN), f32),
            dma((DEPTH,)),
            pltpu.VMEM((2, 2, CODED, WIN), i16),
            dma((2,)),
        ] + tail_scratch(),
        compiler_params=params,
        name="code_grads",
    )(flag, *[in_hbm(grad) for grad in grads])


FINE = 2.0**23


def pack_kernel(own, out):
    for start in range(0, ROWS, 64):
        part = slice(start, start + 64)
        words = [
            jnp.minimum(jnp.round(own[0, comp, part, :] * FINE).astype(jnp.int32), 2**23 - 1) for comp in range(2)
        ]
        both = ((words[0] & 255) << 8) + (words[1] & 255) - 2**15
        for plane, value in enumerate((both, words[0] >> 8, words[1] >> 8)):
            out[plane, part, :] = value.astype(i16)


def pack(own):
    return pl.pallas_call(
        pack_kernel,
        in_specs=[vmem],
        out_specs=vmem,
        out_shape=jax.ShapeDtypeStruct((3, ROWS, COLS), i16),
        compiler_params=params,
        name="pack",
    )(own)


def unpack_kernel(even, odd, out, first, last, buf, sem):
    copies = []
    for i in range(GROUP):
        array = (even, odd)[i % 2]
        for start in range(0, WIN, 64):
            part = slice(start, start + 64)
            both = array[i // 2, 0, part, :].astype(jnp.int32) + 2**15
            for comp, byte in enumerate((both >> 8, both & 255)):
                word = (array[i // 2, 1 + comp, part, :].astype(jnp.int32) << 8) + byte
                buf[i, comp, part, :] = word.astype(f32) * (1.0 / FINE)
                if i in (0, GROUP - 1):
                    (last if i else first)[comp, part, :] = buf[i, comp, part, :]
        copies.append(pltpu.make_async_copy(buf.at[i], out.at[i], sem.at[i]))
        copies[-1].start()
    for copy in copies:
        copy.wait()


def unpack(even, odd):
    return pl.pallas_call(
        unpack_kernel,
        in_specs=[vmem] * 2,
        out_specs=[hbm, vmem, vmem],
        out_shape=[pltpu.HBM((GROUP, 2, WIN, WIN), f32)] + [jax.ShapeDtypeStruct((2, WIN, WIN), f32)] * 2,
        scratch_shapes=[pltpu.VMEM((GROUP, 2, WIN, WIN), f32), dma((GROUP,))],
        compiler_params=params,
        name="unpack",
    )(even, odd)


def corner(place, slot):
    row, col = place[slot, 0], place[slot, 1]
    base = pl.multiple_of((row >> 3) << 3, 8)
    return base, row - base, col


def cut_kernel(place, own, after, out, slab):
    for plane in range(3):
        slab[:ROWS, :] = own[plane].astype(jnp.int32)
        slab[ROWS:, :] = after[plane].astype(jnp.int32)
        for slot in range(CAP):
            base, shift, col = corner(place, slot)
            picked = slab[pl.ds(base, WIN + 8), :]
            picked = pltpu.roll(picked, lax.rem(COLS - col, COLS), 1)[:, :WIN]
            picked = pltpu.roll(picked, lax.rem(WIN + 8 - shift, WIN + 8), 0)[:WIN]
            out[slot, plane] = picked.astype(i16)


def cut_windows(place, own, after):
    return pl.pallas_call(
        cut_kernel,
        in_specs=[smem, vmem, vmem],
        out_specs=vmem,
        out_shape=jax.ShapeDtypeStruct((CAP, 3, WIN, WIN), i16),
        scratch_shapes=[pltpu.VMEM((2 * ROWS, COLS), jnp.int32)],
        compiler_params=params,
        name="cut_windows",
    )(place, own, after)


def add_kernel(place, live, grads, top, low, slab):
    slab[...] = jnp.zeros_like(slab)
    for slot in range(CAP):
        base, shift, col = corner(place, slot)

        @pl.when(slot < live[0])
        def _():
            for comp in range(2):
                own = grads.at[slot, comp]
                tall = jnp.concatenate([decode(own, TOP), decode(own, LOW), jnp.zeros((8, WIN), f32)], axis=0)
                tall = pltpu.roll(tall, shift, 0)
                wide = lanes(tall, jnp.zeros((WIN + 8, COLS - WIN), f32))
                slab[comp, pl.ds(base, WIN + 8), :] += pltpu.roll(wide, col, 1)
    for comp in range(2):
        top[comp] = slab[comp, :ROWS, :]
        encode_plane(low.at[comp], slab[comp, ROWS:ROWS + HALF, :], slab[comp, ROWS + HALF:, :])


def add_windows(place, live, grads):
    return pl.pallas_call(
        add_kernel,
        in_specs=[smem, smem, vmem],
        out_specs=[vmem, vmem],
        out_shape=[
            jax.ShapeDtypeStruct((2, ROWS, COLS), f32),
            jax.ShapeDtypeStruct((2, CODED, COLS), i16),
        ],
        scratch_shapes=[pltpu.VMEM((2, 2 * ROWS, COLS), f32)],
        compiler_params=params,
        name="add_windows",
    )(place, live, grads)


def pick_kernel(core, odd, even, out, sem):
    del even

    @pl.when(core[0] == 1)
    def _():
        copies = [pltpu.make_async_copy(odd.at[i, comp], out.at[i, comp], sem.at[2 * i + comp]) for i in range(4) for comp in range(2)]
        for copy in copies:
            copy.start()
        for copy in copies:
            copy.wait()


def pick_pile(core, even, odd):
    return pl.pallas_call(
        pick_kernel,
        in_specs=[smem, hbm, hbm],
        out_specs=hbm,
        out_shape=grads_shape[0],
        input_output_aliases={2: 0},
        scratch_shapes=[dma((8,))],
        compiler_params=params,
        name="pick_pile",
    )(core, odd, even)


def join_kernel(top, low, out):
    for comp in range(2):
        for part in (TOP, LOW):
            out[0, comp, part, :] = top[comp, part, :] + decode(low.at[comp], part)


def join(top, low):
    return pl.pallas_call(
        join_kernel,
        in_specs=[vmem] * 2,
        out_specs=vmem,
        out_shape=jax.ShapeDtypeStruct((1, 2, ROWS, COLS), f32),
        compiler_params=params,
        name="join",
    )(top, low)


def device(x, z, core):
    return x * GROUP + z * 2 + core


ring = range(4)
def ring_step(value, steps, source, target):
    pairs = [(device(x, z, source), device(x, (z + steps) % 4, target)) for x in ring for z in ring]
    return lax.ppermute(value, "depth", pairs)


rings = [[device(x, z, core) for z in ring] for x in ring for core in range(2)]


def exchange(value):
    return lax.all_to_all(value, "depth", 0, 0, axis_index_groups=rings, tiled=True)


def hop(value, source, target):
    return lax.ppermute(value, "depth", [(device(source, z, 0), device(target, z, 0)) for z in ring])


def body(object_slices, probe_wave, amplitudes, positions, counts):
    depth = lax.axis_index("depth")
    stripe = lax.axis_index("stripe")
    stage = depth // GROUP
    slot = (depth % GROUP) // 2
    core = depth % 2
    dft, chirp, pick = (jnp.asarray(t) for t in make_tables())
    place = lax.dynamic_slice_in_dim(positions, stripe * CAP, CAP, 0)
    live = lax.dynamic_slice_in_dim(counts, stripe, 1, 0)
    works = (core == 0) & (slot < live[0])

    def flag_of(t):
        return (slot + 4 * (works & (stage == t))).astype(jnp.int32)[None]

    own = pack(object_slices)
    after = lax.ppermute(own, "stripe", [(i, (i - 1) % 4) for i in ring])
    even = exchange(cut_windows(place, own, after))
    wins, first, final_win = unpack(even, ring_step(even, 0, 1, 0))

    wave, waves = probe_wave, None
    for t in range(STAGES - 1):
        wave, waves = forward_stage(flag_of(t), wave, wins, chirp, first, waves)
        wave = hop(wave, t, t + 1)
    last_wave = waves[GROUP - 1]
    wave, *grads = turn_stage(flag_of(STAGES - 1), wave, wins, chirp, first, dft, amplitudes, pick)
    for t in reversed(range(STAGES - 1)):
        wave = hop(wave, t + 1, t)
        if t == 0:
            grads = code_grads((4 * (works & (stage > 0))).astype(jnp.int32)[None], grads)
        results = backward_stage(t == 0, flag_of(t), wave, wins, chirp, waves, final_win, last_wave, grads)
        grads = results[-2:]
        wave = results[0]

    pile = pick_pile(core.astype(jnp.int32)[None], grads[0], ring_step(grads[1], 0, 0, 1))
    top, low = add_windows(place, live, exchange(pile))
    return join(top, lax.ppermute(low, "stripe", [(i, (i + 1) % 4) for i in ring]))


def solution(mesh):
    return jax.shard_map(
        body,
        mesh=mesh,
        in_specs=(P("depth", None, "stripe", None), P(), P("stripe", None, None), P(), P()),
        out_specs=P("depth", None, "stripe", None),
        check_vma=False,
    )
```

```python
import numpy as np

import jax
import jax.numpy as jnp
from jax import lax
from jax.experimental import pallas as pl
from jax.experimental.pallas import tpu as pltpu
from jax.sharding import PartitionSpec as P

WIN = 256
HALF = 128
ROWS = 256
COLS = 384
CAP = 4
GROUP = 8
STAGES = 4
CHUNK = 128
smoothing = 0.25
f32 = jnp.float32
bf16 = jnp.bfloat16


def split_np(table):
    high = table.astype(bf16)
    low = (table - high.astype(np.float64)).astype(bf16)
    return high, low


def make_tables():
    n = np.arange(HALF)[:, None]
    k = np.arange(HALF)[None, :]
    tables = []
    for parity in (0, 1):
        angle = -2.0 * np.pi * ((n * (2 * k + parity)) % WIN) / WIN
        c, s = np.cos(angle) / 16.0, np.sin(angle) / 16.0
        full = np.block([[c, s], [-s, c]])
        for table in (full, full.T):
            tables.extend(split_np(table))
    dft = np.stack(tables)
    freq = (((np.arange(WIN) + HALF) % WIN) - HALF).astype(np.float64)
    response = np.fft.ifft(np.exp(-1j * np.pi * freq**2 / (2.0 * WIN)))
    near = response[(n - k) % WIN]
    far = response[(n - k - HALF) % WIN]
    tables = []
    for block in ((near + far) / 2.0, (near - far) / 2.0):
        tables.extend(split_np(np.block([[block.real, block.imag], [-block.imag, block.real]])))
    chirp = np.stack(tables)
    order = np.concatenate([np.arange(0, WIN, 2), np.arange(1, WIN, 2)])
    pick = np.zeros((WIN, WIN))
    pick[np.arange(WIN), order] = 1.0
    return dft, chirp, np.stack([pick, pick.T]).astype(bf16)


SUM, DIFF = 0, 2
EVEN, EVEN_T, ODD, ODD_T = 0, 2, 4, 6


def halves(value):
    high = value.astype(bf16)
    low = (value - high.astype(f32)).astype(bf16)
    return high, low


def mm(a, b):
    return jnp.dot(a, b, preferred_element_type=f32)


def right_mul(data, dft, which):
    high, low = halves(data)
    return mm(high, dft[which]) + mm(low, dft[which]) + mm(high, dft[which + 1])


def left_mul(dft, which, data):
    high, low = halves(data)
    return mm(dft[which], high) + mm(dft[which], low) + mm(dft[which + 1], high)


def lanes(a, b):
    return jnp.concatenate([a, b], axis=1)


def rows(a, b):
    return jnp.concatenate([a, b], axis=0)


def propagate(source, sink, chirp):
    top, low = slice(0, HALF), slice(HALF, WIN)
    re_top, im_top = source(top)
    re_low, im_low = source(low)

    sr, si, dr, di = re_top + re_low, im_top + im_low, re_top - re_low, im_top - im_low
    re, im = rows(sr, dr), rows(si, di)
    scol = right_mul(lanes(re[:, :HALF] + re[:, HALF:], im[:, :HALF] + im[:, HALF:]), chirp, SUM)
    dcol = right_mul(lanes(re[:, :HALF] - re[:, HALF:], im[:, :HALF] - im[:, HALF:]), chirp, DIFF)
    im, re = lanes(scol[:, HALF:], dcol[:, HALF:]), lanes(scol[:, :HALF], dcol[:, :HALF])
    total = left_mul(chirp, SUM, rows(im[:HALF], re[:HALF]))
    diff = left_mul(chirp, DIFF, rows(im[HALF:], re[HALF:]))
    for part, both in ((top, total + diff), (low, total - diff)):
        im, re = both[:HALF], both[HALF:]
        sink(
            part,
            lanes(re[:, :HALF] + re[:, HALF:], re[:, :HALF] - re[:, HALF:]),
            lanes(im[:, :HALF] + im[:, HALF:], im[:, :HALF] - im[:, HALF:]),
        )


def exit_wave(source, sink, dft, mid, pointwise):
    for start in range(0, WIN, CHUNK):
        part = slice(start, start + CHUNK)
        re, im = source(part)
        even = lanes(re[:, :HALF] + re[:, HALF:], im[:, :HALF] + im[:, HALF:])
        odd = lanes(re[:, :HALF] - re[:, HALF:], im[:, :HALF] - im[:, HALF:])
        even = right_mul(even, dft, EVEN)
        odd = right_mul(odd, dft, ODD)
        mid[0, part, :] = lanes(even[:, :HALF], odd[:, :HALF])
        mid[1, part, :] = lanes(even[:, HALF:], odd[:, HALF:])
    re_top, re_low = mid[0, :HALF, :], mid[0, HALF:, :]
    im_top, im_low = mid[1, :HALF, :], mid[1, HALF:, :]
    even = left_mul(dft, EVEN_T, rows(re_top + re_low, im_top + im_low))
    odd = left_mul(dft, ODD_T, rows(re_top - re_low, im_top - im_low))
    even = pointwise(slice(0, HALF), even[:HALF], even[HALF:])
    odd = pointwise(slice(HALF, WIN), odd[:HALF], odd[HALF:])
    even = left_mul(dft, EVEN, rows(*even))
    odd = left_mul(dft, ODD, rows(*odd))
    mid[0, :HALF, :] = even[:HALF] + odd[:HALF]
    mid[0, HALF:, :] = even[:HALF] - odd[:HALF]
    mid[1, :HALF, :] = even[HALF:] + odd[HALF:]
    mid[1, HALF:, :] = even[HALF:] - odd[HALF:]
    for start in range(0, WIN, CHUNK):
        part = slice(start, start + CHUNK)
        re, im = mid[0, part, :], mid[1, part, :]
        even = right_mul(lanes(re[:, :HALF], im[:, :HALF]), dft, EVEN_T)
        odd = right_mul(lanes(re[:, HALF:], im[:, HALF:]), dft, ODD_T)
        total, diff = even + odd, even - odd
        sink(part, lanes(total[:, :HALF], diff[:, :HALF]), lanes(total[:, HALF:], diff[:, HALF:]))


CODED = WIN + 16
i16 = jnp.int16


def exponent(most):
    return jnp.ceil(jnp.log2(jnp.maximum(most, 1e-30)))


def encode(dst, part, value):
    exp = exponent(jnp.max(jnp.abs(value), axis=0, keepdims=True))
    scaled = jnp.round(value * (jnp.exp2(-exp) * 32767.0))
    dst[part, :] = scaled.astype(jnp.int32).astype(i16)
    return jnp.broadcast_to(exp, (8, value.shape[1])).astype(jnp.int32)


def encode_tail(dst, top, low):
    dst[WIN:, :] = jnp.concatenate([top, low], axis=0).astype(i16)


def decode(src, part):
    tail = src[WIN:, :].astype(jnp.int32)[8 * (part.start // HALF):][:1].astype(f32)
    return src[part, :].astype(jnp.int32).astype(f32) * (jnp.exp2(tail) * (1.0 / 32767.0))


TOP, LOW = slice(0, HALF), slice(HALF, WIN)


def encode_plane(dst, top, low):
    encode_tail(dst, encode(dst, TOP, top), encode(dst, LOW, low))


def decode_wave(dst, src):
    for comp in range(2):
        for part in (TOP, LOW):
            dst[comp, part, :] = decode(src.at[comp], part)


def encode_wave(dst, src):
    for comp in range(2):
        encode_plane(dst.at[comp], src[comp, TOP, :], src[comp, LOW, :])


def times(re, im, win, part):
    tr, ti = win[0, part, :], win[1, part, :]
    return re * tr - im * ti, re * ti + im * tr


class Ahead:
    def __init__(self, arrays, buf, sem, depth):
        self.arrays, self.buf, self.sem, self.depth = arrays, buf, sem, depth

    def copy(self, i):
        slot = i & (self.depth - 1)
        return pltpu.make_async_copy(self.arrays.at[i], self.buf.at[slot], self.sem.at[slot])

    def start(self, i):
        self.copy(i).start()

    def wait(self, i):
        self.copy(i).wait()

    def at(self, i):
        return self.buf.at[i & (self.depth - 1)]


class Fetch:
    def __init__(self, pairs, sem):
        self.copies = [pltpu.make_async_copy(src, dst, sem.at[i]) for i, (src, dst) in enumerate(pairs)]

    def start(self):
        for copy in self.copies:
            copy.start()

    def wait(self):
        for copy in self.copies:
            copy.wait()


def forward_slice(src, dst, windows, i, chirp):
    def source(part):
        return times(src[0, part, :], src[1, part, :], windows.at(i), part)

    def sink(part, re, im):
        dst[0, part, :] = re
        dst[1, part, :] = im

    propagate(source, sink, chirp)


def retreat(i, part, re, im, adj, wave, windows, grad, tails):
    wr, wi = wave[0, part, :], wave[1, part, :]
    half = part.start // HALF
    for comp, value in enumerate((wr * re - wi * im, -(wr * im + wi * re))):
        if tails is None:
            grad[comp, part, :] = value
        else:
            tails[comp, 8 * half:8 * half + 8, :] = encode(grad.at[comp], part, value)
    adj[0, part, :], adj[1, part, :] = times(re, im, windows.at(i), part)


def finish_grad(grad, tails):
    for comp in range(2):
        grad[comp, WIN:, :] = tails[comp].astype(i16)


def backward_slice(i, adj, wave, windows, chirp, grad, tails):
    def source(part):
        return adj[0, part, :], adj[1, part, :]

    def sink(part, re, im):
        retreat(i, part, re, im, adj, wave, windows, grad, tails)

    propagate(source, sink, chirp)
    if tails is not None:
        finish_grad(grad, tails)


def copy_wave(dst, src):
    for comp in range(2):
        dst[comp] = src[comp].astype(f32)


def forward_kernel(first, flag, coded, wins, chirp, first_win, *rest):
    wave_out, waves, win_buf, win_sem, buf, sem = rest[-6:]
    windows = Ahead(wins, win_buf, win_sem, win_buf.shape[0])

    def store(i):
        slot = lax.rem(i, 3)
        return pltpu.make_async_copy(buf.at[slot], waves.at[i], sem.at[slot])

    @pl.when(flag[0] >= 4)
    def _():
        for i in range(1, DEPTH - 1):
            windows.start(jnp.int32(i))
        copy_wave(win_buf.at[0], first_win)
        if first:
            copy_wave(buf.at[0], coded)
        else:
            decode_wave(buf.at[0], coded)

        @pl.loop(0, GROUP)
        def _(i):
            @pl.when(i + DEPTH - 1 < GROUP)
            def _():
                windows.start(i + DEPTH - 1)

            store(i).start()

            @pl.when(i >= 2)
            def _():
                store(i - 2).wait()

            @pl.when(i > 0)
            def _():
                windows.wait(i)

            forward_slice(buf.at[lax.rem(i, 3)], buf.at[lax.rem(i + 1, 3)], windows, i, chirp)

        encode_wave(wave_out, buf.at[GROUP % 3])
        store(jnp.int32(GROUP - 2)).wait()
        store(jnp.int32(GROUP - 1)).wait()


class Gradients:
    def __init__(self, grads, buf, sem):
        self.grads, self.buf, self.sem = grads, buf, sem

    def copy(self, i, odd):
        return pltpu.make_async_copy(self.buf.at[odd], self.grads[odd].at[i >> 1], self.sem.at[odd])

    def start(self, i):
        for odd in range(2):
            @pl.when((i & 1) == odd)
            def _():
                self.copy(i, odd).start()

    def wait(self, i):
        for odd in range(2):
            @pl.when((i & 1) == odd)
            def _():
                self.copy(i, odd).wait()


def turn_kernel(flag, coded, wins, chirp, first_win, dft_in, patterns, pick_in, adj_out, *rest):
    *grads, win_buf, win_sem, grad_buf, grad_sem, adj = rest[:7]
    waves, mid, far_amp, dft, pattern, pick, late_sem = rest[7:]
    windows = Ahead(wins, win_buf, win_sem, win_buf.shape[0])
    out = Gradients(grads, grad_buf, grad_sem)
    end = GROUP - 1

    @pl.when(flag[0] >= 4)
    def _():
        for i in range(1, GROUP):
            windows.start(jnp.int32(i))
        copy_wave(win_buf.at[0], first_win)
        late = Fetch([(dft_in, dft), (patterns.at[flag[0] & 3], pattern), (pick_in, pick)], late_sem)
        late.start()
        decode_wave(waves.at[0], coded)

        @pl.loop(0, end)
        def _(i):
            @pl.when(i > 0)
            def _():
                windows.wait(i)

            forward_slice(waves.at[i], waves.at[i + 1], windows, i, chirp)

        windows.wait(jnp.int32(end))
        late.wait()
        picked = mm(pick[0], pattern[...]).astype(bf16)
        far_amp[...] = mm(picked, pick[1])

        def source(part):
            return times(waves[end, 0, part, :], waves[end, 1, part, :], win_buf.at[end], part)

        def exit_point(part, re, im):
            smooth = jnp.sqrt(re * re + im * im + smoothing)
            factor = 1.0 - far_amp[part, :] / smooth
            return factor * re, factor * im

        def sink(part, re, im):
            retreat(end, part, re, -im, adj, waves.at[end], windows, grad_buf.at[end & 1], None)

        exit_wave(source, sink, dft, mid, exit_point)
        out.start(jnp.int32(end))

        @pl.loop(0, end)
        def _(step):
            i = end - 1 - step

            @pl.when(step > 0)
            def _():
                out.wait(i + 2)

            backward_slice(i, adj, waves.at[i], windows, chirp, grad_buf.at[i & 1], None)
            out.start(i)

        encode_wave(adj_out, adj)
        out.wait(jnp.int32(1))
        out.wait(jnp.int32(0))


def backward_kernel(final, flag, coded, wins, chirp, waves, last_win, last_wave, *rest):
    rest = rest[2:]
    if not final:
        adj_out, rest = rest[0], rest[1:]
    *grads, win_buf, win_sem, grad_buf, grad_sem, adj, wave_buf, wave_sem = rest[:9]
    tails = rest[9] if final else None
    windows = Ahead(wins, win_buf, win_sem, win_buf.shape[0])
    out = Gradients(grads, grad_buf, grad_sem)

    kept = Ahead(waves, wave_buf, wave_sem, wave_buf.shape[0])

    @pl.when(flag[0] >= 4)
    def _():
        for i in range(1, DEPTH - 1):
            windows.start(jnp.int32(GROUP - 1 - i))
            kept.start(jnp.int32(GROUP - 1 - i))
        copy_wave(win_buf.at[(GROUP - 1) % DEPTH], last_win)
        copy_wave(wave_buf.at[(GROUP - 1) % DEPTH], last_wave)
        decode_wave(adj, coded)

        @pl.loop(0, GROUP)
        def _(step):
            i = GROUP - 1 - step
            @pl.when(step > 0)
            def _():
                windows.wait(i)
                kept.wait(i)

            @pl.when(i >= DEPTH - 1)
            def _():
                windows.start(i - DEPTH + 1)
                kept.start(i - DEPTH + 1)

            @pl.when(step >= 2)
            def _():
                out.wait(i + 2)

            backward_slice(i, adj, kept.at(i), windows, chirp, grad_buf.at[i & 1], tails)
            out.start(i)

        if not final:
            encode_wave(adj_out, adj)
        out.wait(jnp.int32(1))
        out.wait(jnp.int32(0))


vmem = pl.BlockSpec(memory_space=pltpu.VMEM)
smem = pl.BlockSpec(memory_space=pltpu.SMEM)
hbm = pl.BlockSpec(memory_space=pltpu.HBM)
params = pltpu.CompilerParams(vmem_limit_bytes=24 * 2**20)
wave_shape = jax.ShapeDtypeStruct((2, CODED, WIN), i16)
waves_shape = pltpu.HBM((GROUP, 2, WIN, WIN), f32)
grads_shape = [pltpu.HBM((GROUP // 2, 2, CODED, WIN), i16)] * 2
dma = pltpu.SemaphoreType.DMA
DEPTH = 4
win_scratch = lambda depth: [pltpu.VMEM((depth, 2, WIN, WIN), f32), dma((depth,))]
raw_shape = [pltpu.HBM((GROUP // 2, 2, WIN, WIN), f32)] * 2
grad_scratch = lambda coded: [
    pltpu.VMEM((2, 2, CODED, WIN), i16) if coded else pltpu.VMEM((2, 2, WIN, WIN), f32),
    dma((2,)),
    pltpu.VMEM((2, WIN, WIN), f32),
]
tail_scratch = lambda: [pltpu.VMEM((2, 16, WIN), jnp.int32)]


def in_hbm(value):
    return pltpu.with_memory_space_constraint(value, pltpu.HBM)


def forward_stage(flag, wave, wins, chirp, first_win, waves):
    first = waves is None
    args = [flag, wave, in_hbm(wins), chirp, first_win]
    args += [] if first else [in_hbm(waves)]
    return pl.pallas_call(
        lambda *refs: forward_kernel(first, *refs),
        in_specs=[smem, vmem, hbm, vmem, vmem] + [hbm] * (len(args) - 5),
        out_specs=[vmem, hbm],
        out_shape=[wave_shape, waves_shape],
        input_output_aliases={} if first else {5: 1},
        scratch_shapes=win_scratch(DEPTH) + [
            pltpu.VMEM((3, 2, WIN, WIN), f32),
            dma((3,)),
        ],
        compiler_params=params,
        name="forward_stage",
    )(*args)


def turn_stage(flag, wave, wins, chirp, first_win, dft, patterns, pick):
    return pl.pallas_call(
        turn_kernel,
        in_specs=[smem, vmem, hbm, vmem, vmem] + [hbm] * 3,
        out_specs=[vmem] + [hbm] * 2,
        out_shape=[wave_shape, *raw_shape],
        scratch_shapes=win_scratch(GROUP) + grad_scratch(False) + [
            pltpu.VMEM((GROUP, 2, WIN, WIN), f32),
            pltpu.VMEM((2, WIN, WIN), f32),
            pltpu.VMEM((WIN, WIN), f32),
            pltpu.VMEM((8, WIN, WIN), bf16),
            pltpu.VMEM((WIN, WIN), bf16),
            pltpu.VMEM((2, WIN, WIN), bf16),
            dma((3,)),
        ],
        compiler_params=params,
        name="turn_stage",
    )(flag, wave, in_hbm(wins), chirp, first_win, in_hbm(dft), in_hbm(patterns), in_hbm(pick))


def backward_stage(final, flag, adj, wins, chirp, waves, last_win, last_wave, grads):
    lead = 0 if final else 1
    return pl.pallas_call(
        lambda *refs: backward_kernel(final, *refs),
        in_specs=[smem, vmem, hbm, vmem, hbm, vmem, vmem] + [hbm] * 2,
        out_specs=[vmem] * lead + [hbm] * 2,
        out_shape=[wave_shape] * lead + (grads_shape if final else raw_shape),
        input_output_aliases={7 + k: lead + k for k in range(2)},
        scratch_shapes=win_scratch(DEPTH) + grad_scratch(final) + [
            pltpu.VMEM((DEPTH, 2, WIN, WIN), f32),
            dma((DEPTH,)),
        ] + (tail_scratch() if final else []),
        compiler_params=params,
        name="backward_stage",
    )(flag, adj, in_hbm(wins), chirp, in_hbm(waves), last_win, last_wave, *[in_hbm(grad) for grad in grads])


def code_kernel(flag, even, odd, coded_even, coded_odd, buf, sem, out_buf, out_sem, tails):
    def load(i):
        return pltpu.make_async_copy((even, odd)[i % 2].at[i // 2], buf.at[i % DEPTH], sem.at[i % DEPTH])

    def store(i):
        return pltpu.make_async_copy(
            out_buf.at[i % 2], (coded_even, coded_odd)[i % 2].at[i // 2], out_sem.at[i % 2]
        )

    @pl.when(flag[0] >= 4)
    def _():
        for i in range(DEPTH):
            load(i).start()
        for i in range(GROUP):
            load(i).wait()
            if i >= 2:
                store(i - 2).wait()
            for comp in range(2):
                for half, part in enumerate((TOP, LOW)):
                    tails[comp, 8 * half:8 * half + 8, :] = encode(
                        out_buf.at[i % 2, comp], part, buf[i % DEPTH, comp, part, :]
                    )
            finish_grad(out_buf.at[i % 2], tails)
            store(i).start()
            if i + DEPTH < GROUP:
                load(i + DEPTH).start()
        store(GROUP - 2).wait()
        store(GROUP - 1).wait()


def code_grads(flag, grads):
    return pl.pallas_call(
        code_kernel,
        in_specs=[smem] + [hbm] * 2,
        out_specs=[hbm] * 2,
        out_shape=grads_shape,
        scratch_shapes=[
            pltpu.VMEM((DEPTH, 2, WIN, WIN), f32),
            dma((DEPTH,)),
            pltpu.VMEM((2, 2, CODED, WIN), i16),
            dma((2,)),
        ] + tail_scratch(),
        compiler_params=params,
        name="code_grads",
    )(flag, *[in_hbm(grad) for grad in grads])


FINE = 2.0**23


def pack_kernel(own, out):
    for start in range(0, ROWS, 64):
        part = slice(start, start + 64)
        words = [
            jnp.minimum(jnp.round(own[0, comp, part, :] * FINE).astype(jnp.int32), 2**23 - 1) for comp in range(2)
        ]
        both = ((words[0] & 255) << 8) + (words[1] & 255) - 2**15
        for plane, value in enumerate((both, words[0] >> 8, words[1] >> 8)):
            out[plane, part, :] = value.astype(i16)


def pack(own):
    return pl.pallas_call(
        pack_kernel,
        in_specs=[vmem],
        out_specs=vmem,
        out_shape=jax.ShapeDtypeStruct((3, ROWS, COLS), i16),
        compiler_params=params,
        name="pack",
    )(own)


def unpack_kernel(even, odd_in, out, first, last, buf, sem, odd, odd_sem):
    copies = []
    fetch = Fetch([(odd_in.at[i], odd.at[i]) for i in range(GROUP // 2)], odd_sem)
    fetch.start()
    for i in (*range(0, GROUP, 2), *range(1, GROUP, 2)):
        array = (even, odd)[i % 2]
        if i % 2:
            fetch.copies[i // 2].wait()
        for start in range(0, WIN, 64):
            part = slice(start, start + 64)
            both = array[i // 2, 0, part, :].astype(jnp.int32) + 2**15
            for comp, byte in enumerate((both >> 8, both & 255)):
                word = (array[i // 2, 1 + comp, part, :].astype(jnp.int32) << 8) + byte
                buf[i, comp, part, :] = word.astype(f32) * (1.0 / FINE)
                if i in (0, GROUP - 1):
                    (last if i else first)[comp, part, :] = buf[i, comp, part, :]
        copies.append(pltpu.make_async_copy(buf.at[i], out.at[i], sem.at[i]))
        copies[-1].start()
    for copy in copies:
        copy.wait()


def unpack(even, odd):
    return pl.pallas_call(
        unpack_kernel,
        in_specs=[vmem, hbm],
        out_specs=[hbm, vmem, vmem],
        out_shape=[pltpu.HBM((GROUP, 2, WIN, WIN), f32)] + [jax.ShapeDtypeStruct((2, WIN, WIN), f32)] * 2,
        scratch_shapes=[
            pltpu.VMEM((GROUP, 2, WIN, WIN), f32),
            dma((GROUP,)),
            pltpu.VMEM((GROUP // 2, 3, WIN, WIN), i16),
            dma((GROUP // 2,)),
        ],
        compiler_params=params,
        name="unpack",
    )(even, odd)


def corner(place, slot):
    row, col = place[slot, 0], place[slot, 1]
    base = pl.multiple_of((row >> 3) << 3, 8)
    return base, row - base, col


def cut_kernel(place, own, after, out, slab):
    for plane in range(3):
        slab[:ROWS, :] = own[plane].astype(jnp.int32)
        slab[ROWS:, :] = after[plane].astype(jnp.int32)
        for slot in range(CAP):
            base, shift, col = corner(place, slot)
            picked = slab[pl.ds(base, WIN + 8), :]
            picked = pltpu.roll(picked, lax.rem(COLS - col, COLS), 1)[:, :WIN]
            picked = pltpu.roll(picked, lax.rem(WIN + 8 - shift, WIN + 8), 0)[:WIN]
            out[slot, plane] = picked.astype(i16)


def cut_windows(place, own, after):
    return pl.pallas_call(
        cut_kernel,
        in_specs=[smem, vmem, vmem],
        out_specs=vmem,
        out_shape=jax.ShapeDtypeStruct((CAP, 3, WIN, WIN), i16),
        scratch_shapes=[pltpu.VMEM((2 * ROWS, COLS), jnp.int32)],
        compiler_params=params,
        name="cut_windows",
    )(place, own, after)


def add_kernel(place, live, grads, top, low, slab):
    slab[...] = jnp.zeros_like(slab)
    for slot in range(CAP):
        base, shift, col = corner(place, slot)

        @pl.when(slot < live[0])
        def _():
            for comp in range(2):
                own = grads.at[slot, comp]
                tall = jnp.concatenate([decode(own, TOP), decode(own, LOW), jnp.zeros((8, WIN), f32)], axis=0)
                tall = pltpu.roll(tall, shift, 0)
                wide = lanes(tall, jnp.zeros((WIN + 8, COLS - WIN), f32))
                slab[comp, pl.ds(base, WIN + 8), :] += pltpu.roll(wide, col, 1)
    for comp in range(2):
        top[comp] = slab[comp, :ROWS, :]
        encode_plane(low.at[comp], slab[comp, ROWS:ROWS + HALF, :], slab[comp, ROWS + HALF:, :])


def add_windows(place, live, grads):
    return pl.pallas_call(
        add_kernel,
        in_specs=[smem, smem, vmem],
        out_specs=[vmem, vmem],
        out_shape=[
            jax.ShapeDtypeStruct((2, ROWS, COLS), f32),
            jax.ShapeDtypeStruct((2, CODED, COLS), i16),
        ],
        scratch_shapes=[pltpu.VMEM((2, 2 * ROWS, COLS), f32)],
        compiler_params=params,
        name="add_windows",
    )(place, live, grads)


def pick_kernel(core, odd, even, out, sem):
    del even

    @pl.when(core[0] == 1)
    def _():
        copies = [pltpu.make_async_copy(odd.at[i, comp], out.at[i, comp], sem.at[2 * i + comp]) for i in range(4) for comp in range(2)]
        for copy in copies:
            copy.start()
        for copy in copies:
            copy.wait()


def pick_pile(core, even, odd):
    return pl.pallas_call(
        pick_kernel,
        in_specs=[smem, hbm, hbm],
        out_specs=hbm,
        out_shape=grads_shape[0],
        input_output_aliases={2: 0},
        scratch_shapes=[dma((8,))],
        compiler_params=params,
        name="pick_pile",
    )(core, odd, even)


def join_kernel(top, low, out):
    for comp in range(2):
        for part in (TOP, LOW):
            out[0, comp, part, :] = top[comp, part, :] + decode(low.at[comp], part)


def join(top, low):
    return pl.pallas_call(
        join_kernel,
        in_specs=[vmem] * 2,
        out_specs=vmem,
        out_shape=jax.ShapeDtypeStruct((1, 2, ROWS, COLS), f32),
        compiler_params=params,
        name="join",
    )(top, low)


def device(x, z, core):
    return x * GROUP + z * 2 + core


ring = range(4)
def ring_step(value, steps, source, target):
    pairs = [(device(x, z, source), device(x, (z + steps) % 4, target)) for x in ring for z in ring]
    return lax.ppermute(value, "depth", pairs)


rings = [[device(x, z, core) for z in ring] for x in ring for core in range(2)]


def exchange(value):
    return lax.all_to_all(value, "depth", 0, 0, axis_index_groups=rings, tiled=True)


def hop(value, source, target):
    return lax.ppermute(value, "depth", [(device(source, z, 0), device(target, z, 0)) for z in ring])


def body(object_slices, probe_wave, amplitudes, positions, counts):
    depth = lax.axis_index("depth")
    stripe = lax.axis_index("stripe")
    stage = depth // GROUP
    slot = (depth % GROUP) // 2
    core = depth % 2
    dft, chirp, pick = (jnp.asarray(t) for t in make_tables())
    place = lax.dynamic_slice_in_dim(positions, stripe * CAP, CAP, 0)
    live = lax.dynamic_slice_in_dim(counts, stripe, 1, 0)
    works = (core == 0) & (slot < live[0])

    def flag_of(t):
        return (slot + 4 * (works & (stage == t))).astype(jnp.int32)[None]

    own = pack(object_slices)
    after = lax.ppermute(own, "stripe", [(i, (i - 1) % 4) for i in ring])
    even = exchange(cut_windows(place, own, after))
    wins, first, final_win = unpack(even, ring_step(even, 0, 1, 0))

    wave, waves = probe_wave, None
    for t in range(STAGES - 1):
        wave, waves = forward_stage(flag_of(t), wave, wins, chirp, first, waves)
        wave = hop(wave, t, t + 1)
    last_wave = waves[GROUP - 1]
    wave, *grads = turn_stage(flag_of(STAGES - 1), wave, wins, chirp, first, dft, amplitudes, pick)
    for t in reversed(range(STAGES - 1)):
        wave = hop(wave, t + 1, t)
        if t == 0:
            grads = code_grads((4 * (works & (stage > 0))).astype(jnp.int32)[None], grads)
        results = backward_stage(t == 0, flag_of(t), wave, wins, chirp, waves, final_win, last_wave, grads)
        grads = results[-2:]
        wave = results[0]

    pile = pick_pile(core.astype(jnp.int32)[None], grads[0], ring_step(grads[1], 0, 0, 1))
    top, low = add_windows(place, live, exchange(pile))
    return join(top, lax.ppermute(low, "stripe", [(i, (i + 1) % 4) for i in ring]))


def solution(mesh):
    return jax.shard_map(
        body,
        mesh=mesh,
        in_specs=(P("depth", None, "stripe", None), P(), P("stripe", None, None), P(), P()),
        out_specs=P("depth", None, "stripe", None),
        check_vma=False,
    )
```
